32 devices in a mesh: row: 2 (over core), pitch: 4 (over y, x), span: 4 (over z).
Axes of the slice: x: 2, y: 2, z: 4, core: 2. Of those that a mesh axis runs over, the one named last changes fastest.
Arguments:
- snapshots: bfloat16 [2, 20, 3, 32, 256, 256], P('row', None, None, 'pitch', 'span'), may hold values from -6 to 6
- snap_index: int32 [16], replicated, may hold values from 0 to 19, as said below
- flow_state: float32 [2, 5, 32, 256, 256], P('row', None, 'pitch', 'span'), may hold values from -6 to 6
- eddy_viscosity: float32 [2, 32, 256, 256], P('row', 'pitch', 'span'), may hold values from 0.04 to 0.4
- intersection: int32 [2, 32], P('row'), may hold values from 0 to 31, as said below
- counts: int32 [2, 32], P('row'), may hold values from 1 to 8, as said below
Outputs:
- received_stress: float32 [2, 6, 256, 256], P('row', None, 'span')
- new_state: float32 [2, 5, 32, 256, 256], P('row', None, 'pitch', 'span')
The draws below stay inside these ranges and needn't reach their ends.
Inputs may be any that keep to these rules, and one draw needn't show every extreme that they name: `snap_index`: 16 distinct slots, among them slot 0 and slot 19. `intersection`: for each row, a one-to-one map of blocks. Call blocks k * 8 to (k + 1) * 8 - 1 group k: the blocks of one group take their sources from at most 2 blocks of any one group of the other layout, and exactly 2 for some pairs of groups. `counts`: each row has a block with all 8 cells live.
All inputs are finite; a program needn't handle non-finite values.
Results may differ from the reference program's by a relative error of at most 0.0003.
Values sent between devices are 32-bit elements; how exact they have to be, the bound alone decides.
A program may use at most 128 MiB of HBM per device.

```python
import math
import jax
import jax.numpy as jnp
from jax import lax

ROWS = 2
SNAPS = 16
SLOTS = 20
BLOCK = 8
BLK_DEV = 8
CAPACITY = 2
AXIAL = 256
NPITCH = 32
NSPAN = 256
NBLK = 32


def draw_snap_index(key, part):
    middle = jax.random.permutation(key, SLOTS - 2)[:SNAPS - 2] + 1
    chosen = jnp.concatenate([jnp.array([0, SLOTS - 1], dtype=jnp.int32), middle.astype(jnp.int32)])
    shuffle = jax.random.permutation(jax.random.fold_in(key, 7), SNAPS)
    return chosen[shuffle].astype(jnp.int32)


def draw_intersection(key, part):
    span_count = NBLK // BLK_DEV
    layouts = []
    for row_num in range(ROWS):
        row_key = jax.random.fold_in(key, 11 + row_num)
        offsets_base = jax.random.permutation(jax.random.fold_in(row_key, 1), span_count)[:BLK_DEV // CAPACITY]
        offsets = jnp.repeat(offsets_base, CAPACITY)
        offsets = offsets[jax.random.permutation(jax.random.fold_in(row_key, 2), BLK_DEV)]
        local_order = jax.random.permutation(jax.random.fold_in(row_key, 3), BLK_DEV)
        devices = jnp.arange(span_count, dtype=jnp.int32)
        source_dev = (devices[:, None] - offsets[None, :].astype(jnp.int32)) % span_count
        layouts.append((source_dev * BLK_DEV + local_order[None, :].astype(jnp.int32)).reshape(NBLK).astype(jnp.int32))
    return jnp.stack(layouts)


def draw_counts(key, part):
    values = jax.random.randint(key, (ROWS, NBLK), 1, BLOCK + 1)
    full_spot = jax.random.randint(jax.random.fold_in(key, 5), (ROWS, 1), 0, NBLK)
    return jnp.where(jnp.arange(NBLK)[None, :] == full_spot, BLOCK, values).astype(jnp.int32)


def block_levels(rng, extent, cuts, low, top_value):
    level, own = 1.0, jax.random.fold_in(rng, 6)
    for axis_at, parts in cuts:
        draws = jnp.exp(jax.random.uniform(jax.random.fold_in(own, axis_at), (parts,), jnp.float32, low / len(cuts), top_value / len(cuts)))
        level = level * jnp.repeat(draws, extent[axis_at] // parts).reshape([-1 if axis == axis_at else 1 for axis in range(len(extent))])
    return level


def scatter_about(stream_key, shape, scale, reach, split=(), kind=jnp.bfloat16):
    drawn = scale * jax.random.normal(stream_key, shape, jnp.float32)
    if split:
        drawn = drawn * block_levels(stream_key, shape, split, -0.22, 0.18)
    return jnp.clip(drawn, -reach, reach).astype(kind)


def setup_inputs(seed: int = 0) -> dict:
    seeds = jax.random.split(jax.random.key(seed), 7)
    snapshots = scatter_about(seeds[0], (ROWS, SLOTS, 3, NPITCH, NSPAN, AXIAL), 1.0, 6.0, ((0, 2), (3, 4), (4, 4)))
    snap_index = draw_snap_index(jax.random.fold_in(seeds[6], 71), 0)
    flow_state = scatter_about(seeds[2], (ROWS, 5, NPITCH, NSPAN, AXIAL), 1.0, 6.0, ((0, 2), (2, 4), (3, 4)), jnp.float32)
    eddy_viscosity = jnp.clip(jnp.exp(math.log(0.4) - 2.3025851 * jax.random.uniform(seeds[3], (ROWS, NPITCH, NSPAN, AXIAL), jnp.float32) ** block_levels(seeds[3], (ROWS, NPITCH, NSPAN, AXIAL), ((0, 2), (1, 4), (2, 4)), -0.2, 0.2)), 0.04, 0.4)
    intersection = draw_intersection(jax.random.fold_in(seeds[6], 71), 0)
    counts = draw_counts(jax.random.fold_in(seeds[6], 71), 0)
    return {"snapshots": snapshots, "snap_index": snap_index, "flow_state": flow_state, "eddy_viscosity": eddy_viscosity, "intersection": intersection, "counts": counts}


stress_pairs = ((0, 0), (0, 1), (0, 2), (1, 1), (1, 2), (2, 2))
time_step = 0.1


def axial_diff(values):
    padded = jnp.concatenate([values[..., :1], values, values[..., -1:]], axis=-1)
    return (padded[..., 2:] - padded[..., :-2]) * 0.5


def residual(flow_field, speed, viscosity, live_mask, forcing):
    pitch_pad = jnp.concatenate([flow_field[:, -1:], flow_field, flow_field[:, :1]], axis=1)
    span_pad = jnp.pad(flow_field, ((0, 0), (0, 0), (1, 1), (0, 0)))
    axial_pad = jnp.concatenate([flow_field[..., :1], flow_field, flow_field[..., -1:]], axis=3)
    laplace = (pitch_pad[:, 2:] + pitch_pad[:, :-2] + span_pad[:, :, 2:] + span_pad[:, :, :-2]
               + axial_pad[..., 2:] + axial_pad[..., :-2] - 6.0 * flow_field)
    return live_mask * (-axial_diff(speed * flow_field) + viscosity * laplace + forcing)


def row_stress(snaps_row, snap_index):
    def add_mean(running, slot):
        return running + snaps_row[slot].astype(jnp.float32), None

    zeros_three = jnp.zeros(snaps_row.shape[1:], jnp.float32)
    running, _ = lax.scan(add_mean, zeros_three, snap_index)
    time_mean = running / SNAPS

    def add_products(running, slot):
        fluct = snaps_row[slot].astype(jnp.float32) - time_mean
        products = jnp.stack([fluct[p] * fluct[q] for p, q in stress_pairs])
        return running + products, None

    zeros_six = jnp.zeros((6,) + snaps_row.shape[2:], jnp.float32)
    summed, _ = lax.scan(add_products, zeros_six, snap_index)
    cell_stress = summed / SNAPS
    return time_mean, jnp.sum(cell_stress, axis=1) / NPITCH


def reference(snapshots, snap_index, flow_state, eddy_viscosity, intersection, counts):
    means = []
    averaged = []
    for r in range(ROWS):
        time_mean, pitch_mean = row_stress(snapshots[r], snap_index)
        means.append(time_mean)
        averaged.append(pitch_mean)
    received = []
    for r in range(ROWS):
        source_row = averaged[1 - r].reshape(6, NBLK, BLOCK, AXIAL)
        received.append(jnp.take(source_row, intersection[r], axis=1).reshape(6, NSPAN, AXIAL))
    received_stress = jnp.stack(received)
    span_pos = (jnp.arange(NSPAN, dtype=jnp.float32) + 0.5) / NSPAN
    curvature = (1.0 / (1.0 + span_pos))[:, None]
    results = []
    for r in range(ROWS):
        stress_in = received[r]
        source_x = -axial_diff(stress_in[0]) - curvature * stress_in[1]
        source_r = -axial_diff(stress_in[1]) + curvature * (stress_in[5] - stress_in[3])
        source_t = -axial_diff(stress_in[2]) - 2.0 * curvature * stress_in[4]
        time_mean = means[r]
        energy = time_mean[0] * source_x + time_mean[1] * source_r + time_mean[2] * source_t
        forcing = jnp.concatenate([
            jnp.zeros((1, NPITCH, NSPAN, AXIAL), jnp.float32),
            jnp.broadcast_to(jnp.stack([source_x, source_r, source_t])[:, None], (3, NPITCH, NSPAN, AXIAL)),
            energy[None]], axis=0)
        live_mask = (jnp.arange(BLOCK, dtype=jnp.int32)[None, :] < counts[r][:, None]).astype(jnp.float32)
        live_mask = live_mask.reshape(NSPAN)[:, None]
        speed = 0.5 + time_mean[0]
        viscosity = eddy_viscosity[r]
        start = flow_state[r]
        section_one = start + time_step * residual(start, speed, viscosity, live_mask, forcing)
        results.append(0.5 * (start + section_one + time_step * residual(section_one, speed, viscosity, live_mask, forcing)))
    return received_stress, jnp.stack(results)
```

```python
import functools

import jax
import jax.numpy as jnp
from jax import lax
from jax.experimental import pallas as pl
from jax.experimental.pallas import tpu as pltpu
from jax.sharding import PartitionSpec as P

SNAPS = 16
BLOCK = 8
CAPACITY = 2
LANES = 128
FIRST = 4
ROWS_BF16 = 16
MESH = pl.DeviceIdType.MESH

stress_pairs = ((0, 0), (0, 1), (0, 2), (1, 1), (1, 2), (2, 2))
time_step = 0.1


def stress_tile(snaps, slots, mean, part, j):
    rows = slice(j * ROWS_BF16, (j + 1) * ROWS_BF16)
    cells = mean.shape[1]
    halves = mean.shape[3] // LANES
    for h in range(halves):
        cols = slice(h * LANES, (h + 1) * LANES)

        def one(i, acc):
            def load(t):
                return [snaps[slots[t], c, i, :, cols].astype(jnp.float32) for c in range(3)]

            base = load(0)
            sums, prods = None, None
            for t in range(1, SNAPS):
                now = load(t)
                d = [now[c] - base[c] for c in range(3)]
                pr = [d[p] * d[q] for p, q in stress_pairs]
                sums = d if sums is None else [a + b for a, b in zip(sums, d)]
                prods = pr if prods is None else [a + b for a, b in zip(prods, pr)]
            shift = [s * (1.0 / SNAPS) for s in sums]
            for c in range(3):
                mean[c, i, rows, cols] = base[c] + shift[c]
            return tuple(
                a + (pr - sums[p] * shift[q]) for a, pr, (p, q) in zip(acc, prods, stress_pairs)
            )

        zero = jnp.zeros((ROWS_BF16, LANES), jnp.float32)
        acc = lax.fori_loop(0, cells, one, (zero,) * 6)
        for m in range(6):
            for k in range(2):
                part[m * halves + h, 2 * j + k] = acc[m][k * BLOCK : (k + 1) * BLOCK]
    for u in range(6 * halves, part.shape[0]):
        for k in range(2):
            part[u, 2 * j + k] = jnp.zeros((BLOCK, LANES), jnp.float32)


def next_cell(x):
    lane = lax.broadcasted_iota(jnp.int32, x.shape, 1)
    return jnp.where(lane == x.shape[1] - 1, x, pltpu.roll(x, x.shape[1] - 1, 1))


def last_cell(x):
    lane = lax.broadcasted_iota(jnp.int32, x.shape, 1)
    return jnp.where(lane == 0, x, pltpu.roll(x, 1, 1))


def couple_kernel(
    n_p, n_s, n_x, scale,
    slots_hbm, links_hbm, counts_hbm, snaps_hbm, q_hbm, visc_hbm,
    rec_out, new,
    slot_list, links, counts,
    part, rsy, out_buf, a2a, rec, qpad, spad, face, mean, visc, dtm, src,
    zsend, zrecv,
    ry_s, ry_r, aa_s, aa_r, ax_s, ax_r, ay_s, ay_r, hq_s, hq_r, hs_s, hs_r, hz_s, hz_r,
    loc, snap_sem, *snaps,
):
    r, p, s = lax.axis_index("row"), lax.axis_index("pitch"), lax.axis_index("span")
    comps, cells, span, axial = q_hbm.shape
    n_y = n_p // n_x
    y, x = p // n_x, lax.rem(p, n_x)
    us = part.shape[0] // n_p
    ux = us * n_x
    blocks = span // BLOCK
    halves = axial // LANES
    tile = ROWS_BF16
    top = 8
    tiles = span // tile
    inner = pl.ds(top, span)

    barrier = pltpu.get_barrier_semaphore()

    def greet(*to):
        pl.semaphore_signal(barrier, inc=1, device_id=to, device_id_type=MESH)

    for d in range(1, n_p):
        greet(r, lax.rem(p + d, n_p), s)
    for d in range(n_y):
        greet(1 - r, lax.rem(y + d, n_y) * n_x + x, s)
    for d in range(1, n_s):
        for e in range(n_x):
            greet(r, y * n_x + lax.rem(x + e, n_x), lax.rem(s + d, n_s))

    loads = []
    for k, (a, b) in enumerate(((slots_hbm, slot_list), (links_hbm, links), (counts_hbm, counts))):
        loads.append(pltpu.make_async_copy(a, b, loc.at[2 + k]))
    snap_loads = [
        pltpu.make_async_copy(
            snaps_hbm.at[:, :, :, pl.ds(j * tile, tile)], snaps[j], snap_sem.at[j]
        )
        for j in range(tiles)
    ]
    load_q = pltpu.make_async_copy(q_hbm, qpad.at[:, pl.ds(1, cells), inner], loc.at[0])
    load_visc = pltpu.make_async_copy(visc_hbm, visc, loc.at[1])
    for copy in loads:
        copy.start()
    snap_loads[0].start()
    load_q.start()
    for copy in snap_loads[1:]:
        copy.start()
    load_visc.start()

    pl.semaphore_wait(barrier, n_p - 1 + n_y + n_x * (n_s - 1))

    right, left = lax.rem(p + 1, n_p), lax.rem(p + n_p - 1, n_p)
    above, below = lax.rem(s + 1, n_s), lax.rem(s + n_s - 1, n_s)
    sides = ((cells - 1, 0, right), (0, cells + 1, left))

    def send(a, b, ss, rs, to):
        copy = pltpu.make_async_remote_copy(
            src_ref=a, dst_ref=b, send_sem=ss, recv_sem=rs, device_id=to, device_id_type=MESH
        )
        copy.start()
        return copy

    def q_face(c):
        return [
            send(q_hbm.at[c, mine], qpad.at[c, theirs, inner], hq_s.at[w, c], hq_r.at[w, c], (r, to, s))
            for w, (mine, theirs, to) in enumerate(sides)
        ]

    q_faces = [q_face(c) for c in range(FIRST)]

    def span_faces(pad, k):
        def pack(i, carry):
            for c in range(comps):
                zsend[k, 0, c, pl.ds(i, 1)] = pad[c, i + 1, top + span - 1 : top + span]
                zsend[k, 1, c, pl.ds(i, 1)] = pad[c, i + 1, top : top + 1]
            return carry

        lax.fori_loop(0, cells, pack, 0)
        return [
            send(zsend.at[k, w], zrecv.at[k, w], hz_s.at[k, w], hz_r.at[k, w], (r, p, to))
            for w, to in ((0, above), (1, below))
        ]

    def span_land(pad, k):
        def land(i, carry):
            for c in range(comps):
                row = zrecv[k, 0, c, pl.ds(i, 1)]
                pad[c, i + 1, top - 1 : top] = jnp.where(s == 0, jnp.zeros_like(row), row)
                row = zrecv[k, 1, c, pl.ds(i, 1)]
                pad[c, i + 1, top + span : top + span + 1] = jnp.where(
                    s == n_s - 1, jnp.zeros_like(row), row
                )
            return carry

        lax.fori_loop(0, cells, land, 0)

    load_q.wait()
    q_span = span_faces(qpad, 0)
    for copy in loads:
        copy.wait()

    slots = [slot_list[t] for t in range(SNAPS)]
    to_y = []
    for j in range(tiles):
        snap_loads[j].wait()
        stress_tile(snaps[j], slots, mean, part, j)
        pair = pl.ds(2 * j, 2)
        for d in range(n_y):
            to = lax.rem(y + d, n_y)
            to_y.append(send(
                part.at[pl.ds(to * ux, ux), pair], rsy.at[d, :, pair],
                ry_s.at[d, j], ry_r.at[d, j], (1 - r, to * n_x + x, s),
            ))

    for j in range(tiles):
        row = lax.broadcasted_iota(jnp.int32, (tile, axial), 0)
        first_count = counts[s * blocks + 2 * j]
        second_count = counts[s * blocks + 2 * j + 1]
        limit = jnp.where(row < BLOCK, first_count, second_count + BLOCK)
        dtm[j * tile : (j + 1) * tile] = jnp.where(row < limit, time_step, 0.0).astype(jnp.float32)
    for copy in q_span:
        copy.wait()
    span_land(qpad, 0)
    load_visc.wait()

    def section(pad, i, which, forced, finish, parts=tuple(range(blocks))):
        for j in parts:
            rows = slice(j * BLOCK, (j + 1) * BLOCK)
            nu = visc[i, rows]
            means = [mean[c, i, rows] for c in range(3 if forced and 4 in which else 1)]
            speed = 0.5 + means[0]
            live = dtm[rows]
            ahead = live * (nu - 0.5 * next_cell(speed))
            behind = live * (nu + 0.5 * last_cell(speed))
            nu = live * nu
            at = top + j * BLOCK
            ends = []
            for c in which:
                x = pad[c, i + 1, at : at + BLOCK]
                around = (
                    pad[c, i, at : at + BLOCK] + pad[c, i + 2, at : at + BLOCK]
                    + pad[c, i + 1, at - 1 : at + BLOCK - 1]
                    + pad[c, i + 1, at + 1 : at + BLOCK + 1]
                )
                step = (
                    ahead * next_cell(x) + behind * last_cell(x) + nu * (around - 6.0 * x)
                )
                if forced and 1 <= c <= 3:
                    step = step + src[c - 1, rows]
                if forced and c == 4:
                    step = step + (
                        means[0] * src[0, rows] + means[1] * src[1, rows] + means[2] * src[2, rows]
                    )
                ends.append(x + step)
            for c, end in zip(which, ends):
                finish(c, rows, at, end)

    everything = tuple(range(comps))
    early = tuple(range(comps - 1))
    s_faces = []

    def early_face(c):
        for copy in q_faces[c]:
            copy.wait()

        def one(e, carry):
            i = e * (cells - 1)

            def finish(c, rows, at, end):
                face[e, c, rows] = end

            section(qpad, i, (c,), False, finish)
            return carry

        lax.fori_loop(0, 2, one, 0)

    def early_send(c):
        for w, (mine, theirs, to) in enumerate(sides):
            s_faces.append(send(
                face.at[1 - w, c], spad.at[c, theirs, inner],
                hs_s.at[w, c], hs_r.at[w, c], (r, to, s),
            ))

    def reduce_y():
        for copy in to_y:
            copy.wait()
        exchange = []
        for d in range(n_s):
            to = lax.rem(s + d, n_s)
            count = jnp.int32(0)
            picks = [jnp.int32(0)] * CAPACITY
            for k in range(blocks):
                block = links[to * blocks + k]
                here = block // blocks == s
                inside = block % blocks
                for c in range(CAPACITY):
                    picks[c] = jnp.where(here & (count == c), inside, picks[c])
                count = count + here.astype(jnp.int32)
            for e in range(n_x):
                to_x = lax.rem(x + e, n_x)
                local = d == 0 and e == 0
                for c in range(CAPACITY):
                    for u in range(us):
                        total = rsy[0, to_x * us + u, picks[c]]
                        for f in range(1, n_y):
                            total = total + rsy[f, to_x * us + u, picks[c]]
                        if local:
                            a2a[0, 0, c, u] = total * scale
                        else:
                            out_buf[e, d, c, u] = total * scale
                if not local:
                    exchange.append(send(
                        out_buf.at[e, d], a2a.at[e, d], aa_s.at[e, d], aa_r.at[e, d],
                        (r, y * n_x + to_x, to),
                    ))
        return exchange

    def place(exchange):
        sources = [links[s * blocks + k] // blocks for k in range(blocks)]
        for copy in exchange:
            copy.wait()
        for k in range(blocks):
            slot = jnp.int32(0)
            for e in range(k):
                slot = slot + (sources[e] == sources[k]).astype(jnp.int32)
            slot = jnp.minimum(slot, CAPACITY - 1)
            away = lax.rem(s - sources[k] + n_s, n_s)
            for u in range(us):
                total = a2a[0, away, slot, u]
                for e in range(1, n_x):
                    total = total + a2a[e, away, slot, u]
                rec[p * us + u, k * BLOCK : (k + 1) * BLOCK] = total
        mine = pl.ds(p * us, us)
        over_x = []
        for d in range(1, n_x):
            to = y * n_x + lax.rem(x + d, n_x)
            over_x.append(send(rec.at[mine], rec.at[mine], ax_s.at[d], ax_r.at[d], (r, to, s)))
        over_y = [
            send(rec.at[mine], rec.at[mine], ay_s.at[0, d], ay_r.at[0, d],
                 (r, lax.rem(y + d, n_y) * n_x + x, s))
            for d in range(1, n_y)
        ]
        return over_x, over_y

    def spread(over_x, over_y):
        for d in range(1, n_x):
            over_x[d - 1].wait()
            got = pl.ds((y * n_x + lax.rem(x + n_x - d, n_x)) * us, us)
            for e in range(1, n_y):
                over_y.append(send(
                    rec.at[got], rec.at[got], ay_s.at[d, e], ay_r.at[d, e],
                    (r, lax.rem(y + e, n_y) * n_x + x, s),
                ))
        for copy in over_y:
            copy.wait()

    def sources():
        for j in range(span // tile):
            rows = slice(j * tile, (j + 1) * tile)
            t = [
                jnp.concatenate([rec[m * halves + h, rows] for h in range(halves)], axis=1)
                for m in range(6)
            ]
            for m in range(6):
                rec_out[m, rows] = t[m]
            row = lax.broadcasted_iota(jnp.int32, (tile, axial), 0) + (s * span + j * tile)
            curve = 1.0 / (1.0 + (row.astype(jnp.float32) + 0.5) / (span * n_s))
            diff = [(next_cell(t[m]) - last_cell(t[m])) * 0.5 for m in range(3)]
            live = dtm[rows]
            src[0, rows] = live * (-diff[0] - curve * t[1])
            src[1, rows] = live * (-diff[1] + curve * (t[5] - t[3]))
            src[2, rows] = live * (-diff[2] - 2.0 * curve * t[4])

    rims = (0, blocks - 1)
    middle = tuple(range(1, blocks - 1))

    def first(i, which, parts):
        def finish(c, rows, at, end):
            spad[c, i + 1, at : at + BLOCK] = end

        section(qpad, i, which, True, finish, parts)

    def second(i, which, parts):
        def finish(c, rows, at, end):
            new[c, i, rows] = 0.5 * (qpad[c, i + 1, at : at + BLOCK] + end)

        section(spad, i, which, True, finish, parts)

    def at_edges(part, which, parts):
        def one(e, carry):
            part(e * (cells - 1), which, parts)
            return carry

        lax.fori_loop(0, 2, one, 0)

    def inside(part, parts):
        def one(i, carry):
            part(i, everything, parts)
            return carry

        lax.fori_loop(1, cells - 1, one, 0)

    early_face(0)
    early_face(1)
    step = reduce_y()
    for c in range(FIRST, comps):
        q_faces.append(q_face(c))
    early_send(0)
    step = place(step)
    early_send(1)
    for c in range(2, comps - 1):
        early_face(c)
        early_send(c)
    for copy in q_faces[comps - 1]:
        copy.wait()
    spread(*step)
    sources()
    at_edges(first, (comps - 1,), rims + middle)
    last_faces = [
        send(
            spad.at[comps - 1, mine + 1, inner], spad.at[comps - 1, theirs, inner],
            hs_s.at[w, comps - 1], hs_r.at[w, comps - 1], (r, to, s),
        )
        for w, (mine, theirs, to) in enumerate(sides)
    ]
    at_edges(first, early, rims)
    inside(first, rims)
    s_span = span_faces(spad, 1)
    at_edges(first, early, middle)
    inside(first, middle)
    inside(second, middle)
    for copy in s_span:
        copy.wait()
    span_land(spad, 1)
    inside(second, rims)
    for copy in s_faces:
        copy.wait()

    def force_halo(e, carry):
        for j in range(blocks):
            for c in range(1, comps - 1):
                at = top + j * BLOCK
                old = spad[c, e * (cells + 1), at : at + BLOCK]
                spad[c, e * (cells + 1), at : at + BLOCK] = old + src[c - 1, j * BLOCK : (j + 1) * BLOCK]
        return carry

    lax.fori_loop(0, 2, force_halo, 0)
    at_edges(second, early, rims + middle)
    for copy in last_faces:
        copy.wait()
    at_edges(second, (comps - 1,), rims + middle)


def store_kernel(a, b, a_out, b_out, sems):
    copies = [pltpu.make_async_copy(a, a_out, sems.at[0])]
    for c in range(b.shape[0]):
        copies.append(pltpu.make_async_copy(b.at[c], b_out.at[c], sems.at[1 + c]))
    for copy in copies:
        copy.start()
    for copy in copies:
        copy.wait()


def body(n_p, n_s, snapshots, snap_index, flow_state, eddy_viscosity, intersection, counts):
    start = flow_state[0]
    comps, cells, span, axial = start.shape
    halves = axial // LANES
    us = -(-6 * halves // n_p)
    units = us * n_p
    blocks = span // BLOCK
    tiles = span // ROWS_BF16
    n_x = 2 if n_p % 2 == 0 else 1
    n_y = n_p // n_x
    f32, i32 = jnp.float32, jnp.int32
    pad = (comps, cells + 2, span + 16, axial)
    vmem = pl.BlockSpec(memory_space=pltpu.VMEM)
    hbm = pl.BlockSpec(memory_space=pltpu.HBM)
    dma = pltpu.SemaphoreType.DMA
    operands = (snap_index, intersection[0], counts[0], snapshots[0], start, eddy_viscosity[0])
    operands = [pltpu.with_memory_space_constraint(a, pltpu.HBM) for a in operands]
    rec_shape = (6, span, axial)
    received, new = pl.pallas_call(
        functools.partial(couple_kernel, n_p, n_s, n_x, 1.0 / (SNAPS * cells * n_p)),
        out_shape=(pltpu.VMEM(rec_shape, f32), pltpu.VMEM(start.shape, f32)),
        in_specs=[hbm] * 6,
        out_specs=(vmem, vmem),
        scratch_shapes=[
            pltpu.SMEM(snap_index.shape, i32),
            pltpu.SMEM(intersection.shape[1:], i32),
            pltpu.SMEM(counts.shape[1:], i32),
            pltpu.VMEM((units, blocks, BLOCK, LANES), f32),
            pltpu.VMEM((n_y, us * n_x, blocks, BLOCK, LANES), f32),
            pltpu.VMEM((n_x, n_s, CAPACITY, us, BLOCK, LANES), f32),
            pltpu.VMEM((n_x, n_s, CAPACITY, us, BLOCK, LANES), f32),
            pltpu.VMEM((units, span, LANES), f32),
            pltpu.VMEM(pad, f32),
            pltpu.VMEM(pad, f32),
            pltpu.VMEM((2, comps - 1, span, axial), f32),
            pltpu.VMEM((3, cells, span, axial), f32),
            pltpu.VMEM((cells, span, axial), f32),
            pltpu.VMEM((span, axial), f32),
            pltpu.VMEM((3, span, axial), f32),
            pltpu.VMEM((2, 2, comps, cells, axial), f32),
            pltpu.VMEM((2, 2, comps, cells, axial), f32),
            dma((n_y, tiles)), dma((n_y, tiles)), dma((n_x, n_s)), dma((n_x, n_s)),
            dma((n_x,)), dma((n_x,)),
            dma((n_x, n_y)), dma((n_x, n_y)),
            dma((2, comps)), dma((2, comps)), dma((2, comps)), dma((2, comps)),
            dma((2, 2)), dma((2, 2)), dma((5,)), dma((tiles,)),
        ]
        + [pltpu.VMEM((snapshots.shape[1], 3, cells, ROWS_BF16, axial), snapshots.dtype)] * tiles,
        compiler_params=pltpu.CompilerParams(
            collective_id=0, has_side_effects=True, vmem_limit_bytes=48 * 1024 * 1024
        ),
    )(*operands)
    results = [pltpu.with_memory_space_constraint(a, pltpu.VMEM) for a in (received, new)]
    received, new = pl.pallas_call(
        store_kernel,
        out_shape=(jax.ShapeDtypeStruct(rec_shape, f32), jax.ShapeDtypeStruct(start.shape, f32)),
        in_specs=[vmem, vmem],
        out_specs=(hbm, hbm),
        scratch_shapes=[dma((1 + comps,))],
    )(*results)
    return (received[None], new[None])


def solution(mesh):
    return jax.shard_map(
        functools.partial(body, mesh.shape["pitch"], mesh.shape["span"]),
        mesh=mesh,
        in_specs=(
            P("row", None, None, "pitch", "span", None),
            P(),
            P("row", None, "pitch", "span", None),
            P("row", "pitch", "span", None),
            P("row", None),
            P("row", None),
        ),
        out_specs=(P("row", None, "span", None), P("row", None, "pitch", "span", None)),
        check_vma=False,
    )
```

```python
import functools

import jax
import jax.numpy as jnp
from jax import lax
from jax.experimental import pallas as pl
from jax.experimental.pallas import tpu as pltpu
from jax.sharding import PartitionSpec as P

SNAPS = 16
BLOCK = 8
CAPACITY = 2
LANES = 128
FIRST = 5
AHEAD = 1
ROWS_BF16 = 16
MESH = pl.DeviceIdType.MESH

stress_pairs = ((0, 0), (0, 1), (0, 2), (1, 1), (1, 2), (2, 2))
time_step = 0.1


def stress_tile(snaps, slots, mean, part, j):
    rows = slice(j * ROWS_BF16, (j + 1) * ROWS_BF16)
    cells = mean.shape[1]
    halves = mean.shape[3] // LANES
    for h in range(halves):
        cols = slice(h * LANES, (h + 1) * LANES)

        def one(i, acc):
            def load(t):
                return [snaps[slots[t], c, i, :, cols].astype(jnp.float32) for c in range(3)]

            base = load(0)
            sums, prods = None, None
            for t in range(1, SNAPS):
                now = load(t)
                d = [now[c] - base[c] for c in range(3)]
                pr = [d[p] * d[q] for p, q in stress_pairs]
                sums = d if sums is None else [a + b for a, b in zip(sums, d)]
                prods = pr if prods is None else [a + b for a, b in zip(prods, pr)]
            shift = [s * (1.0 / SNAPS) for s in sums]
            for c in range(3):
                mean[c, i, rows, cols] = base[c] + shift[c]
            return tuple(
                a + (pr - sums[p] * shift[q]) for a, pr, (p, q) in zip(acc, prods, stress_pairs)
            )

        zero = jnp.zeros((ROWS_BF16, LANES), jnp.float32)
        acc = lax.fori_loop(0, cells, one, (zero,) * 6)
        for m in range(6):
            for k in range(2):
                part[m * halves + h, 2 * j + k] = acc[m][k * BLOCK : (k + 1) * BLOCK]
    for u in range(6 * halves, part.shape[0]):
        for k in range(2):
            part[u, 2 * j + k] = jnp.zeros((BLOCK, LANES), jnp.float32)


def next_cell(x):
    lane = lax.broadcasted_iota(jnp.int32, x.shape, 1)
    return jnp.where(lane == x.shape[1] - 1, x, pltpu.roll(x, x.shape[1] - 1, 1))


def last_cell(x):
    lane = lax.broadcasted_iota(jnp.int32, x.shape, 1)
    return jnp.where(lane == 0, x, pltpu.roll(x, 1, 1))


def couple_kernel(
    n_p, n_s, n_x, scale,
    slots_hbm, links_hbm, counts_hbm, snaps_hbm, q_hbm, visc_hbm,
    rec_out, new,
    slot_list, links, counts,
    part, rsy, out_buf, a2a, rec, qpad, spad, face, mean, visc, dtm, src,
    zsend, zrecv,
    ry_s, ry_r, aa_s, aa_r, ax_s, ax_r, ay_s, ay_r, hq_s, hq_r, hs_s, hs_r, hz_s, hz_r,
    loc, snap_sem, later, *snaps,
):
    r, p, s = lax.axis_index("row"), lax.axis_index("pitch"), lax.axis_index("span")
    comps, cells, span, axial = q_hbm.shape
    n_y = n_p // n_x
    y, x = p // n_x, lax.rem(p, n_x)
    us = part.shape[0] // n_p
    ux = us * n_x
    blocks = span // BLOCK
    halves = axial // LANES
    tile = ROWS_BF16
    top = 8
    tiles = span // tile
    inner = pl.ds(top, span)

    barrier = pltpu.get_barrier_semaphore()

    def greet(*to):
        pl.semaphore_signal(barrier, inc=1, device_id=to, device_id_type=MESH)

    for d in range(1, n_p):
        greet(r, lax.rem(p + d, n_p), s)
    for d in range(n_y):
        greet(1 - r, lax.rem(y + d, n_y) * n_x + x, s)
    for d in range(1, n_s):
        @pl.when(s + d < n_s)
        def _():
            for e in range(n_x):
                greet(r, y * n_x + lax.rem(x + e, n_x), s + d)

    loads = []
    for k, (a, b) in enumerate(((slots_hbm, slot_list), (links_hbm, links), (counts_hbm, counts))):
        loads.append(pltpu.make_async_copy(a, b, loc.at[2 + k]))
    snap_loads = [
        pltpu.make_async_copy(
            snaps_hbm.at[:, :, :, pl.ds(j * tile, tile)], snaps[j], snap_sem.at[j]
        )
        for j in range(tiles)
    ]
    load_q = pltpu.make_async_copy(q_hbm, qpad.at[:, pl.ds(1, cells), inner], loc.at[0])
    load_visc = pltpu.make_async_copy(visc_hbm, visc, loc.at[1])
    for copy in loads:
        copy.start()
    for copy in snap_loads:
        copy.start()
    load_q.start()
    load_visc.start()

    pl.semaphore_wait(barrier, n_p - 1 + n_y + n_x * s)
    for d in range(1, n_s):
        @pl.when(s >= d)
        def _():
            for e in range(n_x):
                pl.semaphore_signal(
                    later, inc=1, device_id=(r, y * n_x + lax.rem(x + e, n_x), s - d),
                    device_id_type=MESH,
                )


    right, left = lax.rem(p + 1, n_p), lax.rem(p + n_p - 1, n_p)
    above, below = lax.rem(s + 1, n_s), lax.rem(s + n_s - 1, n_s)
    sides = ((cells - 1, 0, right), (0, cells + 1, left))

    def send(a, b, ss, rs, to):
        copy = pltpu.make_async_remote_copy(
            src_ref=a, dst_ref=b, send_sem=ss, recv_sem=rs, device_id=to, device_id_type=MESH
        )
        copy.start()
        return copy

    def q_face(c):
        return [
            send(q_hbm.at[c, mine], qpad.at[c, theirs, inner], hq_s.at[w, c], hq_r.at[w, c], (r, to, s))
            for w, (mine, theirs, to) in enumerate(sides)
        ]

    q_faces = [q_face(c) for c in range(FIRST)]

    def span_faces(pad, k):
        def pack(i, carry):
            for c in range(comps):
                zsend[k, 0, c, pl.ds(i, 1)] = pad[c, i + 1, top + span - 1 : top + span]
                zsend[k, 1, c, pl.ds(i, 1)] = pad[c, i + 1, top : top + 1]
            return carry

        lax.fori_loop(0, cells, pack, 0)
        return [
            send(zsend.at[k, w], zrecv.at[k, w], hz_s.at[k, w], hz_r.at[k, w], (r, p, to))
            for w, to in ((0, above), (1, below))
        ]

    def span_land(pad, k):
        def land(i, carry):
            for c in range(comps):
                row = zrecv[k, 0, c, pl.ds(i, 1)]
                pad[c, i + 1, top - 1 : top] = jnp.where(s == 0, jnp.zeros_like(row), row)
                row = zrecv[k, 1, c, pl.ds(i, 1)]
                pad[c, i + 1, top + span : top + span + 1] = jnp.where(
                    s == n_s - 1, jnp.zeros_like(row), row
                )
            return carry

        lax.fori_loop(0, cells, land, 0)

    for copy in loads:
        copy.wait()

    slots = [slot_list[t] for t in range(SNAPS)]
    to_y = []
    for j in range(tiles):
        snap_loads[j].wait()
        stress_tile(snaps[j], slots, mean, part, j)
        pair = pl.ds(2 * j, 2)
        for d in range(n_y):
            to = lax.rem(y + d, n_y)
            to_y.append(send(
                part.at[pl.ds(to * ux, ux), pair], rsy.at[d, :, pair],
                ry_s.at[d, j], ry_r.at[d, j], (1 - r, to * n_x + x, s),
            ))

    for j in range(tiles):
        row = lax.broadcasted_iota(jnp.int32, (tile, axial), 0)
        first_count = counts[s * blocks + 2 * j]
        second_count = counts[s * blocks + 2 * j + 1]
        limit = jnp.where(row < BLOCK, first_count, second_count + BLOCK)
        dtm[j * tile : (j + 1) * tile] = jnp.where(row < limit, time_step, 0.0).astype(jnp.float32)
    load_q.wait()

    @pl.when(s < n_s - 1)
    def _():
        pl.semaphore_wait(later, n_x * (n_s - 1 - s))

    q_span = span_faces(qpad, 0)

    def section(pad, i, which, forced, finish, parts=tuple(range(blocks))):
        for j in parts:
            rows = slice(j * BLOCK, (j + 1) * BLOCK)
            nu = visc[i, rows]
            means = [mean[c, i, rows] for c in range(3 if forced and 4 in which else 1)]
            speed = 0.5 + means[0]
            live = dtm[rows]
            ahead = live * (nu - 0.5 * next_cell(speed))
            behind = live * (nu + 0.5 * last_cell(speed))
            nu = live * nu
            at = top + j * BLOCK
            ends = []
            for c in which:
                x = pad[c, i + 1, at : at + BLOCK]
                around = (
                    pad[c, i, at : at + BLOCK] + pad[c, i + 2, at : at + BLOCK]
                    + pad[c, i + 1, at - 1 : at + BLOCK - 1]
                    + pad[c, i + 1, at + 1 : at + BLOCK + 1]
                )
                step = (
                    ahead * next_cell(x) + behind * last_cell(x) + nu * (around - 6.0 * x)
                )
                if forced and 1 <= c <= 3:
                    step = step + src[c - 1, rows]
                if forced and c == 4:
                    step = step + (
                        means[0] * src[0, rows] + means[1] * src[1, rows] + means[2] * src[2, rows]
                    )
                ends.append(x + step)
            for c, end in zip(which, ends):
                finish(c, rows, at, end)

    everything = tuple(range(comps))
    early = tuple(range(comps - 1))
    moved = early[1:]
    s_faces = []

    def early_face(c):
        for copy in q_faces[c]:
            copy.wait()

        def one(e, carry):
            i = e * (cells - 1)

            def finish(c, rows, at, end):
                face[e, c, rows] = end
                spad[c, i + 1, at : at + BLOCK] = end

            section(qpad, i, (c,), False, finish)
            return carry

        lax.fori_loop(0, 2, one, 0)

    def early_send(c):
        for w, (mine, theirs, to) in enumerate(sides):
            s_faces.append(send(
                face.at[1 - w, c], spad.at[c, theirs, inner],
                hs_s.at[w, c], hs_r.at[w, c], (r, to, s),
            ))

    def reduce_y():
        for copy in to_y:
            copy.wait()
        exchange = []
        for d in range(n_s):
            to = lax.rem(s + d, n_s)
            count = jnp.int32(0)
            picks = [jnp.int32(0)] * CAPACITY
            for k in range(blocks):
                block = links[to * blocks + k]
                here = block // blocks == s
                inside = block % blocks
                for c in range(CAPACITY):
                    picks[c] = jnp.where(here & (count == c), inside, picks[c])
                count = count + here.astype(jnp.int32)
            for e in range(n_x):
                to_x = lax.rem(x + e, n_x)
                local = d == 0 and e == 0
                for c in range(CAPACITY):
                    for u in range(us):
                        total = rsy[0, to_x * us + u, picks[c]]
                        for f in range(1, n_y):
                            total = total + rsy[f, to_x * us + u, picks[c]]
                        if local:
                            a2a[0, 0, c, u] = total * scale
                        else:
                            out_buf[e, d, c, u] = total * scale
                if not local:
                    exchange.append(send(
                        out_buf.at[e, d], a2a.at[e, d], aa_s.at[e, d], aa_r.at[e, d],
                        (r, y * n_x + to_x, to),
                    ))
        return exchange

    def place(exchange):
        sources = [links[s * blocks + k] // blocks for k in range(blocks)]
        for copy in exchange:
            copy.wait()
        for k in range(blocks):
            slot = jnp.int32(0)
            for e in range(k):
                slot = slot + (sources[e] == sources[k]).astype(jnp.int32)
            slot = jnp.minimum(slot, CAPACITY - 1)
            away = lax.rem(s - sources[k] + n_s, n_s)
            for u in range(us):
                total = a2a[0, away, slot, u]
                for e in range(1, n_x):
                    total = total + a2a[e, away, slot, u]
                rec[p * us + u, k * BLOCK : (k + 1) * BLOCK] = total
        over_x, over_y = [], []
        for u in range(us):
            mine = pl.ds(p * us + u, 1)
            for d in range(1, n_x):
                to = y * n_x + lax.rem(x + d, n_x)
                over_x.append(send(
                    rec.at[mine], rec.at[mine], ax_s.at[d, u], ax_r.at[d, u], (r, to, s)
                ))
        mine = pl.ds(p * us, us)
        for d in range(1, n_y):
            to = lax.rem(y + d, n_y) * n_x + x
            over_y.append(send(
                rec.at[mine], rec.at[mine], ay_s.at[0, d, 0], ay_r.at[0, d, 0], (r, to, s)
            ))
        return over_x, over_y

    def spread(over_x, over_y):
        for u in range(us):
            for d in range(1, n_x):
                over_x[u * (n_x - 1) + d - 1].wait()
                got = pl.ds((y * n_x + lax.rem(x + n_x - d, n_x)) * us + u, 1)
                for e in range(1, n_y):
                    to = lax.rem(y + e, n_y) * n_x + x
                    over_y.append(send(
                        rec.at[got], rec.at[got], ay_s.at[d, e, u], ay_r.at[d, e, u], (r, to, s)
                    ))
        for copy in over_y:
            copy.wait()

    def sources():
        for j in range(span // tile):
            rows = slice(j * tile, (j + 1) * tile)
            t = [
                jnp.concatenate([rec[m * halves + h, rows] for h in range(halves)], axis=1)
                for m in range(6)
            ]
            for m in range(6):
                rec_out[m, rows] = t[m]
            row = lax.broadcasted_iota(jnp.int32, (tile, axial), 0) + (s * span + j * tile)
            curve = 1.0 / (1.0 + (row.astype(jnp.float32) + 0.5) / (span * n_s))
            diff = [(next_cell(t[m]) - last_cell(t[m])) * 0.5 for m in range(3)]
            live = dtm[rows]
            src[0, rows] = live * (-diff[0] - curve * t[1])
            src[1, rows] = live * (-diff[1] + curve * (t[5] - t[3]))
            src[2, rows] = live * (-diff[2] - 2.0 * curve * t[4])

    rims = (0, blocks - 1)
    middle = tuple(range(1, blocks - 1))

    def first(i, which, parts):
        def finish(c, rows, at, end):
            spad[c, i + 1, at : at + BLOCK] = end

        section(qpad, i, which, False, finish, parts)

    def force(i, which, parts):
        for j in parts:
            rows = slice(j * BLOCK, (j + 1) * BLOCK)
            at = top + j * BLOCK
            for c in which:
                if 1 <= c <= 3:
                    more = src[c - 1, rows]
                else:
                    more = mean[0, i, rows] * src[0, rows]
                    for k in range(1, 3):
                        more = more + mean[k, i, rows] * src[k, rows]
                old = spad[c, i + 1, at : at + BLOCK]
                spad[c, i + 1, at : at + BLOCK] = old + more

    def second(i, which, parts):
        def finish(c, rows, at, end):
            new[c, i, rows] = 0.5 * (qpad[c, i + 1, at : at + BLOCK] + end)

        section(spad, i, which, True, finish, parts)

    def at_edges(part, which, parts):
        def one(e, carry):
            part(e * (cells - 1), which, parts)
            return carry

        lax.fori_loop(0, 2, one, 0)

    def inside(part, parts, which=everything):
        def one(i, carry):
            part(i, which, parts)
            return carry

        lax.fori_loop(1, cells - 1, one, 0)

    step = reduce_y()
    for c in range(FIRST, comps):
        q_faces.append(q_face(c))
    for copy in q_span:
        copy.wait()
    span_land(qpad, 0)
    load_visc.wait()
    for c in range(AHEAD):
        early_face(c)
        early_send(c)
    inside(first, rims + middle)
    step = place(step)
    for c in range(AHEAD, comps - 1):
        early_face(c)
        early_send(c)
    for copy in q_faces[comps - 1]:
        copy.wait()
    at_edges(first, (comps - 1,), rims + middle)
    spread(*step)
    sources()
    at_edges(force, (comps - 1,), rims + middle)
    last_faces = [
        send(
            spad.at[comps - 1, mine + 1, inner], spad.at[comps - 1, theirs, inner],
            hs_s.at[w, comps - 1], hs_r.at[w, comps - 1], (r, to, s),
        )
        for w, (mine, theirs, to) in enumerate(sides)
    ]
    at_edges(force, moved, rims)
    inside(force, rims, moved + (comps - 1,))
    s_span = span_faces(spad, 1)
    at_edges(force, moved, middle)
    inside(force, middle, moved + (comps - 1,))
    inside(second, middle)
    for copy in s_span:
        copy.wait()
    span_land(spad, 1)
    inside(second, rims)
    for copy in s_faces:
        copy.wait()

    def force_halo(e, carry):
        for j in range(blocks):
            for c in range(1, comps - 1):
                at = top + j * BLOCK
                old = spad[c, e * (cells + 1), at : at + BLOCK]
                spad[c, e * (cells + 1), at : at + BLOCK] = old + src[c - 1, j * BLOCK : (j + 1) * BLOCK]
        return carry

    lax.fori_loop(0, 2, force_halo, 0)
    at_edges(second, early, rims + middle)
    for copy in last_faces:
        copy.wait()
    at_edges(second, (comps - 1,), rims + middle)


def store_kernel(a, b, a_out, b_out, sems):
    copies = [pltpu.make_async_copy(a, a_out, sems.at[0])]
    for c in range(b.shape[0]):
        copies.append(pltpu.make_async_copy(b.at[c], b_out.at[c], sems.at[1 + c]))
    for copy in copies:
        copy.start()
    for copy in copies:
        copy.wait()


def body(n_p, n_s, snapshots, snap_index, flow_state, eddy_viscosity, intersection, counts):
    start = flow_state[0]
    comps, cells, span, axial = start.shape
    halves = axial // LANES
    us = -(-6 * halves // n_p)
    units = us * n_p
    blocks = span // BLOCK
    tiles = span // ROWS_BF16
    n_x = 2 if n_p % 2 == 0 else 1
    n_y = n_p // n_x
    f32, i32 = jnp.float32, jnp.int32
    pad = (comps, cells + 2, span + 16, axial)
    vmem = pl.BlockSpec(memory_space=pltpu.VMEM)
    hbm = pl.BlockSpec(memory_space=pltpu.HBM)
    dma = pltpu.SemaphoreType.DMA
    operands = (snap_index, intersection[0], counts[0], snapshots[0], start, eddy_viscosity[0])
    operands = [pltpu.with_memory_space_constraint(a, pltpu.HBM) for a in operands]
    rec_shape = (6, span, axial)
    received, new = pl.pallas_call(
        functools.partial(couple_kernel, n_p, n_s, n_x, 1.0 / (SNAPS * cells * n_p)),
        out_shape=(pltpu.VMEM(rec_shape, f32), pltpu.VMEM(start.shape, f32)),
        in_specs=[hbm] * 6,
        out_specs=(vmem, vmem),
        scratch_shapes=[
            pltpu.SMEM(snap_index.shape, i32),
            pltpu.SMEM(intersection.shape[1:], i32),
            pltpu.SMEM(counts.shape[1:], i32),
            pltpu.VMEM((units, blocks, BLOCK, LANES), f32),
            pltpu.VMEM((n_y, us * n_x, blocks, BLOCK, LANES), f32),
            pltpu.VMEM((n_x, n_s, CAPACITY, us, BLOCK, LANES), f32),
            pltpu.VMEM((n_x, n_s, CAPACITY, us, BLOCK, LANES), f32),
            pltpu.VMEM((units, span, LANES), f32),
            pltpu.VMEM(pad, f32),
            pltpu.VMEM(pad, f32),
            pltpu.VMEM((2, comps - 1, span, axial), f32),
            pltpu.VMEM((3, cells, span, axial), f32),
            pltpu.VMEM((cells, span, axial), f32),
            pltpu.VMEM((span, axial), f32),
            pltpu.VMEM((3, span, axial), f32),
            pltpu.VMEM((2, 2, comps, cells, axial), f32),
            pltpu.VMEM((2, 2, comps, cells, axial), f32),
            dma((n_y, tiles)), dma((n_y, tiles)), dma((n_x, n_s)), dma((n_x, n_s)),
            dma((n_x, us)), dma((n_x, us)), dma((n_x, n_y, us)), dma((n_x, n_y, us)),
            dma((2, comps)), dma((2, comps)), dma((2, comps)), dma((2, comps)),
            dma((2, 2)), dma((2, 2)), dma((5,)), dma((tiles,)), pltpu.SemaphoreType.REGULAR,
        ]
        + [pltpu.VMEM((snapshots.shape[1], 3, cells, ROWS_BF16, axial), snapshots.dtype)] * tiles,
        compiler_params=pltpu.CompilerParams(
            collective_id=0, has_side_effects=True, vmem_limit_bytes=48 * 1024 * 1024
        ),
    )(*operands)
    results = [pltpu.with_memory_space_constraint(a, pltpu.VMEM) for a in (received, new)]
    received, new = pl.pallas_call(
        store_kernel,
        out_shape=(jax.ShapeDtypeStruct(rec_shape, f32), jax.ShapeDtypeStruct(start.shape, f32)),
        in_specs=[vmem, vmem],
        out_specs=(hbm, hbm),
        scratch_shapes=[dma((1 + comps,))],
    )(*results)
    return (received[None], new[None])


def solution(mesh):
    return jax.shard_map(
        functools.partial(body, mesh.shape["pitch"], mesh.shape["span"]),
        mesh=mesh,
        in_specs=(
            P("row", None, None, "pitch", "span", None),
            P(),
            P("row", None, "pitch", "span", None),
            P("row", "pitch", "span", None),
            P("row", None),
            P("row", None),
        ),
        out_specs=(P("row", None, "span", None), P("row", None, "pitch", "span", None)),
        check_vma=False,
    )
```

```python
import functools

import jax
import jax.numpy as jnp
from jax import lax
from jax.experimental import pallas as pl
from jax.experimental.pallas import tpu as pltpu
from jax.sharding import PartitionSpec as P

SNAPS = 16
BLOCK = 8
CAPACITY = 2
LANES = 128
FIRST = 5
ROWS_BF16 = 16
MESH = pl.DeviceIdType.MESH

stress_pairs = ((0, 0), (0, 1), (0, 2), (1, 1), (1, 2), (2, 2))
time_step = 0.1


def stress_tile(snaps, slots, mean, part, j):
    rows = slice(j * ROWS_BF16, (j + 1) * ROWS_BF16)
    cells = mean.shape[1]
    halves = mean.shape[3] // LANES
    for h in range(halves):
        cols = slice(h * LANES, (h + 1) * LANES)

        def one(i, acc):
            def load(t):
                return [snaps[slots[t], c, i, :, cols].astype(jnp.float32) for c in range(3)]

            base = load(0)
            sums, prods = None, None
            for t in range(1, SNAPS):
                now = load(t)
                d = [now[c] - base[c] for c in range(3)]
                pr = [d[p] * d[q] for p, q in stress_pairs]
                sums = d if sums is None else [a + b for a, b in zip(sums, d)]
                prods = pr if prods is None else [a + b for a, b in zip(prods, pr)]
            shift = [s * (1.0 / SNAPS) for s in sums]
            for c in range(3):
                mean[c, i, rows, cols] = base[c] + shift[c]
            return tuple(
                a + (pr - sums[p] * shift[q]) for a, pr, (p, q) in zip(acc, prods, stress_pairs)
            )

        zero = jnp.zeros((ROWS_BF16, LANES), jnp.float32)
        acc = lax.fori_loop(0, cells, one, (zero,) * 6)
        for m in range(6):
            for k in range(2):
                part[m * halves + h, 2 * j + k] = acc[m][k * BLOCK : (k + 1) * BLOCK]
    for u in range(6 * halves, part.shape[0]):
        for k in range(2):
            part[u, 2 * j + k] = jnp.zeros((BLOCK, LANES), jnp.float32)


def next_cell(x):
    lane = lax.broadcasted_iota(jnp.int32, x.shape, 1)
    return jnp.where(lane == x.shape[1] - 1, x, pltpu.roll(x, x.shape[1] - 1, 1))


def last_cell(x):
    lane = lax.broadcasted_iota(jnp.int32, x.shape, 1)
    return jnp.where(lane == 0, x, pltpu.roll(x, 1, 1))


def couple_kernel(
    n_p, n_s, n_x, scale,
    slots_hbm, links_hbm, counts_hbm, snaps_hbm, q_hbm, visc_hbm,
    rec_out, new,
    slot_list, links, counts,
    part, rsy, out_buf, a2a, rec, qpad, spad, face, mean, visc, dtm, src,
    zsend, zrecv,
    ry_s, ry_r, aa_s, aa_r, ax_s, ax_r, ay_s, ay_r, hq_s, hq_r, hs_s, hs_r, hz_s, hz_r,
    loc, snap_sem, later, *snaps,
):
    r, p, s = lax.axis_index("row"), lax.axis_index("pitch"), lax.axis_index("span")
    comps, cells, span, axial = q_hbm.shape
    n_y = n_p // n_x
    y, x = p // n_x, lax.rem(p, n_x)
    us = part.shape[0] // n_p
    ux = us * n_x
    blocks = span // BLOCK
    halves = axial // LANES
    tile = ROWS_BF16
    top = 8
    tiles = span // tile
    inner = pl.ds(top, span)

    barrier = pltpu.get_barrier_semaphore()

    def greet(*to):
        pl.semaphore_signal(barrier, inc=1, device_id=to, device_id_type=MESH)

    for d in range(1, n_p):
        greet(r, lax.rem(p + d, n_p), s)
    for d in range(n_y):
        greet(1 - r, lax.rem(y + d, n_y) * n_x + x, s)
    for d in range(1, n_s):
        @pl.when(s + d < n_s)
        def _():
            for e in range(n_x):
                greet(r, y * n_x + lax.rem(x + e, n_x), s + d)

    loads = []
    for k, (a, b) in enumerate(((slots_hbm, slot_list), (links_hbm, links), (counts_hbm, counts))):
        loads.append(pltpu.make_async_copy(a, b, loc.at[2 + k]))
    snap_loads = [
        pltpu.make_async_copy(
            snaps_hbm.at[:, :, :, pl.ds(j * tile, tile)], snaps[j], snap_sem.at[j]
        )
        for j in range(tiles)
    ]
    load_q = pltpu.make_async_copy(q_hbm, qpad.at[:, pl.ds(1, cells), inner], loc.at[0])
    load_visc = pltpu.make_async_copy(visc_hbm, visc, loc.at[1])
    for copy in loads:
        copy.start()
    for copy in snap_loads:
        copy.start()
    load_q.start()
    load_visc.start()

    pl.semaphore_wait(barrier, n_p - 1 + n_y + n_x * s)
    for d in range(1, n_s):
        @pl.when(s >= d)
        def _():
            for e in range(n_x):
                pl.semaphore_signal(
                    later, inc=1, device_id=(r, y * n_x + lax.rem(x + e, n_x), s - d),
                    device_id_type=MESH,
                )


    right, left = lax.rem(p + 1, n_p), lax.rem(p + n_p - 1, n_p)
    above, below = lax.rem(s + 1, n_s), lax.rem(s + n_s - 1, n_s)
    sides = ((cells - 1, 0, right), (0, cells + 1, left))

    def send(a, b, ss, rs, to):
        copy = pltpu.make_async_remote_copy(
            src_ref=a, dst_ref=b, send_sem=ss, recv_sem=rs, device_id=to, device_id_type=MESH
        )
        copy.start()
        return copy

    def q_face(c):
        return [
            send(q_hbm.at[c, mine], qpad.at[c, theirs, inner], hq_s.at[w, c], hq_r.at[w, c], (r, to, s))
            for w, (mine, theirs, to) in enumerate(sides)
        ]

    q_faces = [q_face(c) for c in range(FIRST)]

    span_sides = ((0, above, s < n_s - 1, s > 0), (1, below, s > 0, s < n_s - 1))
    for w, _, _, got in span_sides:
        @pl.when(jnp.logical_not(got))
        def _():
            for k in range(2):
                for c in range(comps):
                    zrecv[k, w, c] = jnp.zeros((cells, axial), jnp.float32)

    def span_faces(pad, k):
        def pack(i, carry):
            for c in range(comps):
                zsend[k, 0, c, pl.ds(i, 1)] = pad[c, i + 1, top + span - 1 : top + span]
                zsend[k, 1, c, pl.ds(i, 1)] = pad[c, i + 1, top : top + 1]
            return carry

        lax.fori_loop(0, cells, pack, 0)
        copies = []
        for w, to, sent, got in span_sides:
            copy = pltpu.make_async_remote_copy(
                src_ref=zsend.at[k, w], dst_ref=zrecv.at[k, w],
                send_sem=hz_s.at[k, w], recv_sem=hz_r.at[k, w],
                device_id=(r, p, to), device_id_type=MESH,
            )
            pl.when(sent)(copy.start)
            copies.append((copy, sent, got))
        return copies

    def span_wait(copies):
        for copy, sent, got in copies:
            pl.when(sent)(copy.wait_send)
            pl.when(got)(copy.wait_recv)

    def span_land(pad, k):
        def land(i, carry):
            for c in range(comps):
                pad[c, i + 1, top - 1 : top] = zrecv[k, 0, c, pl.ds(i, 1)]
                pad[c, i + 1, top + span : top + span + 1] = zrecv[k, 1, c, pl.ds(i, 1)]
            return carry

        lax.fori_loop(0, cells, land, 0)

    for copy in loads:
        copy.wait()

    slots = [slot_list[t] for t in range(SNAPS)]
    to_y = []
    for j in range(tiles):
        snap_loads[j].wait()
        stress_tile(snaps[j], slots, mean, part, j)
        pair = pl.ds(2 * j, 2)
        for d in range(n_y):
            to = lax.rem(y + d, n_y)
            to_y.append(send(
                part.at[pl.ds(to * ux, ux), pair], rsy.at[d, :, pair],
                ry_s.at[d, j], ry_r.at[d, j], (1 - r, to * n_x + x, s),
            ))

    for j in range(tiles):
        row = lax.broadcasted_iota(jnp.int32, (tile, axial), 0)
        first_count = counts[s * blocks + 2 * j]
        second_count = counts[s * blocks + 2 * j + 1]
        limit = jnp.where(row < BLOCK, first_count, second_count + BLOCK)
        dtm[j * tile : (j + 1) * tile] = jnp.where(row < limit, time_step, 0.0).astype(jnp.float32)
    load_q.wait()

    @pl.when(s < n_s - 1)
    def _():
        pl.semaphore_wait(later, n_x * (n_s - 1 - s))

    q_span = span_faces(qpad, 0)

    def section(pad, i, which, forced, finish, parts=tuple(range(blocks))):
        for j in parts:
            rows = slice(j * BLOCK, (j + 1) * BLOCK)
            nu = visc[i, rows]
            means = [mean[c, i, rows] for c in range(3 if forced and 4 in which else 1)]
            speed = 0.5 + means[0]
            live = dtm[rows]
            ahead = live * (nu - 0.5 * next_cell(speed))
            behind = live * (nu + 0.5 * last_cell(speed))
            nu = live * nu
            at = top + j * BLOCK
            ends = []
            for c in which:
                x = pad[c, i + 1, at : at + BLOCK]
                around = (
                    pad[c, i, at : at + BLOCK] + pad[c, i + 2, at : at + BLOCK]
                    + pad[c, i + 1, at - 1 : at + BLOCK - 1]
                    + pad[c, i + 1, at + 1 : at + BLOCK + 1]
                )
                step = (
                    ahead * next_cell(x) + behind * last_cell(x) + nu * (around - 6.0 * x)
                )
                if forced and 1 <= c <= 3:
                    step = step + src[c - 1, rows]
                if forced and c == 4:
                    step = step + (
                        means[0] * src[0, rows] + means[1] * src[1, rows] + means[2] * src[2, rows]
                    )
                ends.append(x + step)
            for c, end in zip(which, ends):
                finish(c, rows, at, end)

    everything = tuple(range(comps))
    early = tuple(range(comps - 1))
    moved = early[1:]
    s_faces = []

    def early_face(c):
        for copy in q_faces[c]:
            copy.wait()

        def one(e, carry):
            i = e * (cells - 1)

            def finish(c, rows, at, end):
                face[e, c, rows] = end
                spad[c, i + 1, at : at + BLOCK] = end

            section(qpad, i, (c,), False, finish)
            return carry

        lax.fori_loop(0, 2, one, 0)

    def early_send(c, chosen=(0, 1)):
        for w in chosen:
            mine, theirs, to = sides[w]
            s_faces.append(send(
                face.at[1 - w, c], spad.at[c, theirs, inner],
                hs_s.at[w, c], hs_r.at[w, c], (r, to, s),
            ))

    def reduce_y():
        for copy in to_y:
            copy.wait()
        exchange = []
        for d in range(n_s):
            to = lax.rem(s + d, n_s)
            count = jnp.int32(0)
            picks = [jnp.int32(0)] * CAPACITY
            for k in range(blocks):
                block = links[to * blocks + k]
                here = block // blocks == s
                inside = block % blocks
                for c in range(CAPACITY):
                    picks[c] = jnp.where(here & (count == c), inside, picks[c])
                count = count + here.astype(jnp.int32)
            for e in range(n_x):
                to_x = lax.rem(x + e, n_x)
                local = d == 0 and e == 0
                for c in range(CAPACITY):
                    for u in range(us):
                        total = rsy[0, to_x * us + u, picks[c]]
                        for f in range(1, n_y):
                            total = total + rsy[f, to_x * us + u, picks[c]]
                        if local:
                            a2a[0, 0, c, u] = total * scale
                        else:
                            out_buf[e, d, c, u] = total * scale
                if not local:
                    exchange.append(send(
                        out_buf.at[e, d], a2a.at[e, d], aa_s.at[e, d], aa_r.at[e, d],
                        (r, y * n_x + to_x, to),
                    ))
        return exchange

    def place(exchange):
        sources = [links[s * blocks + k] // blocks for k in range(blocks)]
        for copy in exchange:
            copy.wait()
        for k in range(blocks):
            slot = jnp.int32(0)
            for e in range(k):
                slot = slot + (sources[e] == sources[k]).astype(jnp.int32)
            slot = jnp.minimum(slot, CAPACITY - 1)
            away = lax.rem(s - sources[k] + n_s, n_s)
            for u in range(us):
                total = a2a[0, away, slot, u]
                for e in range(1, n_x):
                    total = total + a2a[e, away, slot, u]
                rec[p * us + u, k * BLOCK : (k + 1) * BLOCK] = total
        over_x, over_y = [], []
        for u in range(us):
            mine = pl.ds(p * us + u, 1)
            for d in range(1, n_x):
                to = y * n_x + lax.rem(x + d, n_x)
                over_x.append(send(
                    rec.at[mine], rec.at[mine], ax_s.at[d, u], ax_r.at[d, u], (r, to, s)
                ))
        mine = pl.ds(p * us, us)
        for d in range(1, n_y):
            to = lax.rem(y + d, n_y) * n_x + x
            over_y.append(send(
                rec.at[mine], rec.at[mine], ay_s.at[0, d, 0], ay_r.at[0, d, 0], (r, to, s)
            ))
        return over_x, over_y

    def spread(over_x, over_y):
        for u in range(us):
            for d in range(1, n_x):
                over_x[u * (n_x - 1) + d - 1].wait()
                got = pl.ds((y * n_x + lax.rem(x + n_x - d, n_x)) * us + u, 1)
                for e in range(1, n_y):
                    to = lax.rem(y + e, n_y) * n_x + x
                    over_y.append(send(
                        rec.at[got], rec.at[got], ay_s.at[d, e, u], ay_r.at[d, e, u], (r, to, s)
                    ))
        for copy in over_y:
            copy.wait()

    def sources(parts):
        for j in parts:
            rows = slice(j * BLOCK, (j + 1) * BLOCK)
            t = [
                jnp.concatenate([rec[m * halves + h, rows] for h in range(halves)], axis=1)
                for m in range(6)
            ]
            row = lax.broadcasted_iota(jnp.int32, (BLOCK, axial), 0) + (s * span + j * BLOCK)
            curve = 1.0 / (1.0 + (row.astype(jnp.float32) + 0.5) / (span * n_s))
            diff = [(next_cell(t[m]) - last_cell(t[m])) * 0.5 for m in range(3)]
            live = dtm[rows]
            src[0, rows] = live * (-diff[0] - curve * t[1])
            src[1, rows] = live * (-diff[1] + curve * (t[5] - t[3]))
            src[2, rows] = live * (-diff[2] - 2.0 * curve * t[4])

    rims = (0, blocks - 1)
    middle = tuple(range(1, blocks - 1))

    def first(i, which, parts):
        def finish(c, rows, at, end):
            spad[c, i + 1, at : at + BLOCK] = end

        section(qpad, i, which, False, finish, parts)

    def force(i, which, parts):
        for j in parts:
            rows = slice(j * BLOCK, (j + 1) * BLOCK)
            at = top + j * BLOCK
            for c in which:
                if 1 <= c <= 3:
                    more = src[c - 1, rows]
                else:
                    more = mean[0, i, rows] * src[0, rows]
                    for k in range(1, 3):
                        more = more + mean[k, i, rows] * src[k, rows]
                old = spad[c, i + 1, at : at + BLOCK]
                spad[c, i + 1, at : at + BLOCK] = old + more

    def second(i, which, parts):
        def finish(c, rows, at, end):
            new[c, i, rows] = 0.5 * (qpad[c, i + 1, at : at + BLOCK] + end)

        section(spad, i, which, True, finish, parts)

    def at_edges(part, which, parts):
        def one(e, carry):
            part(e * (cells - 1), which, parts)
            return carry

        lax.fori_loop(0, 2, one, 0)

    def inside(part, parts, which=everything):
        def one(i, carry):
            part(i, which, parts)
            return carry

        lax.fori_loop(1, cells - 1, one, 0)

    step = reduce_y()
    for c in range(FIRST, comps):
        q_faces.append(q_face(c))
    span_wait(q_span)
    span_land(qpad, 0)
    load_visc.wait()
    early_face(0)
    early_face(1)
    early_send(0)
    early_send(1, (0,))
    inside(first, rims + middle)
    step = place(step)
    early_send(1, (1,))
    for c in range(2, comps - 1):
        early_face(c)
        early_send(c)
    for copy in q_faces[comps - 1]:
        copy.wait()
    at_edges(first, (comps - 1,), rims + middle)
    spread(*step)
    def force_halo(e, carry):
        for j in range(blocks):
            for c in range(1, comps - 1):
                at = top + j * BLOCK
                old = spad[c, e * (cells + 1), at : at + BLOCK]
                spad[c, e * (cells + 1), at : at + BLOCK] = old + src[c - 1, j * BLOCK : (j + 1) * BLOCK]
        return carry

    sources(rims)
    at_edges(force, moved + (comps - 1,), rims)
    inside(force, rims, moved + (comps - 1,))
    s_span = span_faces(spad, 1)
    sources(middle)
    at_edges(force, (comps - 1,), middle)
    last_faces = []
    for near in (right < left, right > left):
        w = jnp.where(near, 0, 1)
        last_faces.append(send(
            spad.at[comps - 1, jnp.where(near, cells, 1), inner],
            spad.at[comps - 1, jnp.where(near, 0, cells + 1), inner],
            hs_s.at[w, comps - 1], hs_r.at[w, comps - 1], (r, jnp.where(near, right, left), s),
        ))
    at_edges(force, moved, middle)
    inside(force, middle, moved + (comps - 1,))
    inside(second, middle)
    for m in range(6):
        for h in range(halves):
            rec_out[m, :, h * LANES : (h + 1) * LANES] = rec[m * halves + h]
    for copy in s_faces:
        copy.wait()
    lax.fori_loop(0, 2, force_halo, 0)
    at_edges(second, early, middle)
    span_wait(s_span)
    span_land(spad, 1)
    inside(second, rims)
    at_edges(second, early, rims)
    for copy in last_faces:
        copy.wait()
    at_edges(second, (comps - 1,), rims + middle)


def store_kernel(a, b, a_out, b_out, sems):
    copies = [pltpu.make_async_copy(a, a_out, sems.at[0])]
    for c in range(b.shape[0]):
        copies.append(pltpu.make_async_copy(b.at[c], b_out.at[c], sems.at[1 + c]))
    for copy in copies:
        copy.start()
    for copy in copies:
        copy.wait()


def body(n_p, n_s, snapshots, snap_index, flow_state, eddy_viscosity, intersection, counts):
    start = flow_state[0]
    comps, cells, span, axial = start.shape
    halves = axial // LANES
    us = -(-6 * halves // n_p)
    units = us * n_p
    blocks = span // BLOCK
    tiles = span // ROWS_BF16
    n_x = 2 if n_p % 2 == 0 else 1
    n_y = n_p // n_x
    f32, i32 = jnp.float32, jnp.int32
    pad = (comps, cells + 2, span + 16, axial)
    vmem = pl.BlockSpec(memory_space=pltpu.VMEM)
    hbm = pl.BlockSpec(memory_space=pltpu.HBM)
    dma = pltpu.SemaphoreType.DMA
    operands = (snap_index, intersection[0], counts[0], snapshots[0], start, eddy_viscosity[0])
    operands = [pltpu.with_memory_space_constraint(a, pltpu.HBM) for a in operands]
    rec_shape = (6, span, axial)
    received, new = pl.pallas_call(
        functools.partial(couple_kernel, n_p, n_s, n_x, 1.0 / (SNAPS * cells * n_p)),
        out_shape=(pltpu.VMEM(rec_shape, f32), pltpu.VMEM(start.shape, f32)),
        in_specs=[hbm] * 6,
        out_specs=(vmem, vmem),
        scratch_shapes=[
            pltpu.SMEM(snap_index.shape, i32),
            pltpu.SMEM(intersection.shape[1:], i32),
            pltpu.SMEM(counts.shape[1:], i32),
            pltpu.VMEM((units, blocks, BLOCK, LANES), f32),
            pltpu.VMEM((n_y, us * n_x, blocks, BLOCK, LANES), f32),
            pltpu.VMEM((n_x, n_s, CAPACITY, us, BLOCK, LANES), f32),
            pltpu.VMEM((n_x, n_s, CAPACITY, us, BLOCK, LANES), f32),
            pltpu.VMEM((units, span, LANES), f32),
            pltpu.VMEM(pad, f32),
            pltpu.VMEM(pad, f32),
            pltpu.VMEM((2, comps - 1, span, axial), f32),
            pltpu.VMEM((3, cells, span, axial), f32),
            pltpu.VMEM((cells, span, axial), f32),
            pltpu.VMEM((span, axial), f32),
            pltpu.VMEM((3, span, axial), f32),
            pltpu.VMEM((2, 2, comps, cells, axial), f32),
            pltpu.VMEM((2, 2, comps, cells, axial), f32),
            dma((n_y, tiles)), dma((n_y, tiles)), dma((n_x, n_s)), dma((n_x, n_s)),
            dma((n_x, us)), dma((n_x, us)), dma((n_x, n_y, us)), dma((n_x, n_y, us)),
            dma((2, comps)), dma((2, comps)), dma((2, comps)), dma((2, comps)),
            dma((2, 2)), dma((2, 2)), dma((5,)), dma((tiles,)), pltpu.SemaphoreType.REGULAR,
        ]
        + [pltpu.VMEM((snapshots.shape[1], 3, cells, ROWS_BF16, axial), snapshots.dtype)] * tiles,
        compiler_params=pltpu.CompilerParams(
            collective_id=0, has_side_effects=True, vmem_limit_bytes=48 * 1024 * 1024
        ),
    )(*operands)
    results = [pltpu.with_memory_space_constraint(a, pltpu.VMEM) for a in (received, new)]
    received, new = pl.pallas_call(
        store_kernel,
        out_shape=(jax.ShapeDtypeStruct(rec_shape, f32), jax.ShapeDtypeStruct(start.shape, f32)),
        in_specs=[vmem, vmem],
        out_specs=(hbm, hbm),
        scratch_shapes=[dma((1 + comps,))],
    )(*results)
    return (received[None], new[None])


def solution(mesh):
    return jax.shard_map(
        functools.partial(body, mesh.shape["pitch"], mesh.shape["span"]),
        mesh=mesh,
        in_specs=(
            P("row", None, None, "pitch", "span", None),
            P(),
            P("row", None, "pitch", "span", None),
            P("row", "pitch", "span", None),
            P("row", None),
            P("row", None),
        ),
        out_specs=(P("row", None, "span", None), P("row", None, "pitch", "span", None)),
        check_vma=False,
    )
```

```python
import functools

import jax
import jax.numpy as jnp
from jax import lax
from jax.experimental import pallas as pl
from jax.experimental.pallas import tpu as pltpu
from jax.sharding import PartitionSpec as P

SNAPS = 16
BLOCK = 8
CAPACITY = 2
LANES = 128
FIRST = 5
ROWS_BF16 = 16
MESH = pl.DeviceIdType.MESH

stress_pairs = ((0, 0), (0, 1), (0, 2), (1, 1), (1, 2), (2, 2))
time_step = 0.1


def stress_tile(snaps, slots, mean, part, j):
    rows = slice(j * ROWS_BF16, (j + 1) * ROWS_BF16)
    cells = mean.shape[1]
    halves = mean.shape[3] // LANES
    for h in range(halves):
        cols = slice(h * LANES, (h + 1) * LANES)

        def one(i, acc):
            def load(t):
                return [snaps[slots[t], c, i, :, cols].astype(jnp.float32) for c in range(3)]

            base = load(0)
            sums, prods = None, None
            for t in range(1, SNAPS):
                now = load(t)
                d = [now[c] - base[c] for c in range(3)]
                pr = [d[p] * d[q] for p, q in stress_pairs]
                sums = d if sums is None else [a + b for a, b in zip(sums, d)]
                prods = pr if prods is None else [a + b for a, b in zip(prods, pr)]
            shift = [s * (1.0 / SNAPS) for s in sums]
            for c in range(3):
                mean[c, i, rows, cols] = base[c] + shift[c]
            return tuple(
                a + (pr - sums[p] * shift[q]) for a, pr, (p, q) in zip(acc, prods, stress_pairs)
            )

        zero = jnp.zeros((ROWS_BF16, LANES), jnp.float32)
        acc = lax.fori_loop(0, cells, one, (zero,) * 6)
        for m in range(6):
            for k in range(2):
                part[m * halves + h, 2 * j + k] = acc[m][k * BLOCK : (k + 1) * BLOCK]
    for u in range(6 * halves, part.shape[0]):
        for k in range(2):
            part[u, 2 * j + k] = jnp.zeros((BLOCK, LANES), jnp.float32)


def next_cell(x):
    lane = lax.broadcasted_iota(jnp.int32, x.shape, 1)
    return jnp.where(lane == x.shape[1] - 1, x, pltpu.roll(x, x.shape[1] - 1, 1))


def last_cell(x):
    lane = lax.broadcasted_iota(jnp.int32, x.shape, 1)
    return jnp.where(lane == 0, x, pltpu.roll(x, 1, 1))


def couple_kernel(
    n_p, n_s, n_x, scale,
    slots_hbm, links_hbm, counts_hbm, snaps_hbm, q_hbm, visc_hbm,
    rec_out, new,
    slot_list, links, counts,
    part, rsy, out_buf, a2a, rec, qpad, spad, face, mean, visc, dtm, src,
    zsend, zrecv,
    ry_s, ry_r, aa_s, aa_r, ax_s, ax_r, ay_s, ay_r, hq_s, hq_r, hs_s, hs_r, hz_s, hz_r,
    loc, snap_sem, later, *snaps,
):
    r, p, s = lax.axis_index("row"), lax.axis_index("pitch"), lax.axis_index("span")
    comps, cells, span, axial = q_hbm.shape
    n_y = n_p // n_x
    y, x = p // n_x, lax.rem(p, n_x)
    us = part.shape[0] // n_p
    ux = us * n_x
    blocks = span // BLOCK
    halves = axial // LANES
    tile = ROWS_BF16
    top = 8
    tiles = span // tile
    inner = pl.ds(top, span)

    barrier = pltpu.get_barrier_semaphore()

    def greet(*to):
        pl.semaphore_signal(barrier, inc=1, device_id=to, device_id_type=MESH)

    for d in range(1, n_p):
        greet(r, lax.rem(p + d, n_p), s)
    for d in range(n_y):
        greet(1 - r, lax.rem(y + d, n_y) * n_x + x, s)
    for d in range(1, n_s):
        @pl.when(s + d < n_s)
        def _():
            for e in range(n_x):
                greet(r, y * n_x + lax.rem(x + e, n_x), s + d)

    loads = []
    for k, (a, b) in enumerate(((slots_hbm, slot_list), (links_hbm, links), (counts_hbm, counts))):
        loads.append(pltpu.make_async_copy(a, b, loc.at[2 + k]))
    snap_loads = [
        pltpu.make_async_copy(
            snaps_hbm.at[:, :, :, pl.ds(j * tile, tile)], snaps[j], snap_sem.at[j]
        )
        for j in range(tiles)
    ]
    load_q = pltpu.make_async_copy(q_hbm, qpad.at[:, pl.ds(1, cells), inner], loc.at[0])
    load_visc = pltpu.make_async_copy(visc_hbm, visc, loc.at[1])
    for copy in loads:
        copy.start()
    for copy in snap_loads:
        copy.start()
    load_q.start()
    load_visc.start()

    pl.semaphore_wait(barrier, n_p - 1 + n_y + n_x * s)
    for d in range(1, n_s):
        @pl.when(s >= d)
        def _():
            for e in range(n_x):
                pl.semaphore_signal(
                    later, inc=1, device_id=(r, y * n_x + lax.rem(x + e, n_x), s - d),
                    device_id_type=MESH,
                )


    right, left = lax.rem(p + 1, n_p), lax.rem(p + n_p - 1, n_p)
    above, below = lax.rem(s + 1, n_s), lax.rem(s + n_s - 1, n_s)
    sides = ((cells - 1, 0, right), (0, cells + 1, left))

    def send(a, b, ss, rs, to):
        copy = pltpu.make_async_remote_copy(
            src_ref=a, dst_ref=b, send_sem=ss, recv_sem=rs, device_id=to, device_id_type=MESH
        )
        copy.start()
        return copy

    def q_face(c):
        return [
            send(q_hbm.at[c, mine], qpad.at[c, theirs, inner], hq_s.at[w, c], hq_r.at[w, c], (r, to, s))
            for w, (mine, theirs, to) in enumerate(sides)
        ]

    q_faces = [q_face(c) for c in range(FIRST)]

    span_sides = ((0, above, s < n_s - 1, s > 0), (1, below, s > 0, s < n_s - 1))
    for w, _, _, got in span_sides:
        @pl.when(jnp.logical_not(got))
        def _():
            for k in range(2):
                for c in range(comps):
                    zrecv[k, w, c] = jnp.zeros((cells, axial), jnp.float32)

    def span_faces(pad, k):
        def pack(i, carry):
            for c in range(comps):
                zsend[k, 0, c, pl.ds(i, 1)] = pad[c, i + 1, top + span - 1 : top + span]
                zsend[k, 1, c, pl.ds(i, 1)] = pad[c, i + 1, top : top + 1]
            return carry

        lax.fori_loop(0, cells, pack, 0)
        copies = []
        for w, to, sent, got in span_sides:
            copy = pltpu.make_async_remote_copy(
                src_ref=zsend.at[k, w], dst_ref=zrecv.at[k, w],
                send_sem=hz_s.at[k, w], recv_sem=hz_r.at[k, w],
                device_id=(r, p, to), device_id_type=MESH,
            )
            pl.when(sent)(copy.start)
            copies.append((copy, sent, got))
        return copies

    def span_wait(copies):
        for copy, sent, got in copies:
            pl.when(sent)(copy.wait_send)
            pl.when(got)(copy.wait_recv)

    def span_land(pad, k):
        def land(i, carry):
            for c in range(comps):
                pad[c, i + 1, top - 1 : top] = zrecv[k, 0, c, pl.ds(i, 1)]
                pad[c, i + 1, top + span : top + span + 1] = zrecv[k, 1, c, pl.ds(i, 1)]
            return carry

        lax.fori_loop(0, cells, land, 0)

    for copy in loads:
        copy.wait()

    slots = [slot_list[t] for t in range(SNAPS)]
    to_y = []
    for j in range(tiles):
        snap_loads[j].wait()
        stress_tile(snaps[j], slots, mean, part, j)
        pair = pl.ds(2 * j, 2)
        for d in range(n_y):
            to = lax.rem(y + d, n_y)
            to_y.append(send(
                part.at[pl.ds(to * ux, ux), pair], rsy.at[d, :, pair],
                ry_s.at[d, j], ry_r.at[d, j], (1 - r, to * n_x + x, s),
            ))

    for j in range(tiles):
        row = lax.broadcasted_iota(jnp.int32, (tile, axial), 0)
        first_count = counts[s * blocks + 2 * j]
        second_count = counts[s * blocks + 2 * j + 1]
        limit = jnp.where(row < BLOCK, first_count, second_count + BLOCK)
        dtm[j * tile : (j + 1) * tile] = jnp.where(row < limit, time_step, 0.0).astype(jnp.float32)
    load_q.wait()

    @pl.when(s < n_s - 1)
    def _():
        pl.semaphore_wait(later, n_x * (n_s - 1 - s))

    q_span = span_faces(qpad, 0)

    def section(pad, i, which, forced, finish, parts=tuple(range(blocks))):
        for j in parts:
            rows = slice(j * BLOCK, (j + 1) * BLOCK)
            nu = visc[i, rows]
            means = [mean[c, i, rows] for c in range(3 if forced and 4 in which else 1)]
            speed = 0.5 + means[0]
            live = dtm[rows]
            ahead = live * (nu - 0.5 * next_cell(speed))
            behind = live * (nu + 0.5 * last_cell(speed))
            nu = live * nu
            at = top + j * BLOCK
            ends = []
            for c in which:
                x = pad[c, i + 1, at : at + BLOCK]
                around = (
                    pad[c, i, at : at + BLOCK] + pad[c, i + 2, at : at + BLOCK]
                    + pad[c, i + 1, at - 1 : at + BLOCK - 1]
                    + pad[c, i + 1, at + 1 : at + BLOCK + 1]
                )
                step = (
                    ahead * next_cell(x) + behind * last_cell(x) + nu * (around - 6.0 * x)
                )
                if forced and 1 <= c <= 3:
                    step = step + src[c - 1, rows]
                if forced and c == 4:
                    step = step + (
                        means[0] * src[0, rows] + means[1] * src[1, rows] + means[2] * src[2, rows]
                    )
                ends.append(x + step)
            for c, end in zip(which, ends):
                finish(c, rows, at, end)

    everything = tuple(range(comps))
    early = tuple(range(comps - 1))
    moved = early[1:]
    s_faces = []

    def early_face(c):
        for copy in q_faces[c]:
            copy.wait()

        def one(e, carry):
            i = e * (cells - 1)

            def finish(c, rows, at, end):
                face[e, c, rows] = end
                spad[c, i + 1, at : at + BLOCK] = end

            section(qpad, i, (c,), False, finish)
            return carry

        lax.fori_loop(0, 2, one, 0)

    def early_send(c, chosen=(0, 1)):
        for w in chosen:
            mine, theirs, to = sides[w]
            s_faces.append(send(
                face.at[1 - w, c], spad.at[c, theirs, inner],
                hs_s.at[w, c], hs_r.at[w, c], (r, to, s),
            ))

    def reduce_y():
        for copy in to_y:
            copy.wait()
        exchange = []
        for d in range(n_s):
            to = lax.rem(s + d, n_s)
            count = jnp.int32(0)
            picks = [jnp.int32(0)] * CAPACITY
            for k in range(blocks):
                block = links[to * blocks + k]
                here = block // blocks == s
                inside = block % blocks
                for c in range(CAPACITY):
                    picks[c] = jnp.where(here & (count == c), inside, picks[c])
                count = count + here.astype(jnp.int32)
            for e in range(n_x):
                to_x = lax.rem(x + e, n_x)
                local = d == 0 and e == 0
                for c in range(CAPACITY):
                    for u in range(us):
                        total = rsy[0, to_x * us + u, picks[c]]
                        for f in range(1, n_y):
                            total = total + rsy[f, to_x * us + u, picks[c]]
                        if local:
                            a2a[0, 0, c, u] = total * scale
                        else:
                            out_buf[e, d, c, u] = total * scale
                if not local:
                    exchange.append(send(
                        out_buf.at[e, d], a2a.at[e, d], aa_s.at[e, d], aa_r.at[e, d],
                        (r, y * n_x + to_x, to),
                    ))
        return exchange

    def place(exchange):
        sources = [links[s * blocks + k] // blocks for k in range(blocks)]
        for copy in exchange:
            copy.wait()
        for k in range(blocks):
            slot = jnp.int32(0)
            for e in range(k):
                slot = slot + (sources[e] == sources[k]).astype(jnp.int32)
            slot = jnp.minimum(slot, CAPACITY - 1)
            away = lax.rem(s - sources[k] + n_s, n_s)
            for u in range(us):
                total = a2a[0, away, slot, u]
                for e in range(1, n_x):
                    total = total + a2a[e, away, slot, u]
                rec[p * us + u, k * BLOCK : (k + 1) * BLOCK] = total
        over_x, over_y = [], []
        for u in range(us):
            mine = pl.ds(p * us + u, 1)
            for d in range(1, n_x):
                to = y * n_x + lax.rem(x + d, n_x)
                over_x.append(send(
                    rec.at[mine], rec.at[mine], ax_s.at[d, u], ax_r.at[d, u], (r, to, s)
                ))
        mine = pl.ds(p * us, us)
        for d in range(1, n_y):
            to = lax.rem(y + d, n_y) * n_x + x
            over_y.append(send(
                rec.at[mine], rec.at[mine], ay_s.at[0, d, 0], ay_r.at[0, d, 0], (r, to, s)
            ))
        return over_x, over_y

    def spread(over_x, over_y):
        for u in range(us):
            for d in range(1, n_x):
                over_x[u * (n_x - 1) + d - 1].wait()
                got = pl.ds((y * n_x + lax.rem(x + n_x - d, n_x)) * us + u, 1)
                for e in range(1, n_y):
                    to = lax.rem(y + e, n_y) * n_x + x
                    over_y.append(send(
                        rec.at[got], rec.at[got], ay_s.at[d, e, u], ay_r.at[d, e, u], (r, to, s)
                    ))
        for copy in over_y:
            copy.wait()

    def sources(parts):
        for j in parts:
            rows = slice(j * BLOCK, (j + 1) * BLOCK)
            t = [
                jnp.concatenate([rec[m * halves + h, rows] for h in range(halves)], axis=1)
                for m in range(6)
            ]
            row = lax.broadcasted_iota(jnp.int32, (BLOCK, axial), 0) + (s * span + j * BLOCK)
            curve = 1.0 / (1.0 + (row.astype(jnp.float32) + 0.5) / (span * n_s))
            diff = [(next_cell(t[m]) - last_cell(t[m])) * 0.5 for m in range(3)]
            live = dtm[rows]
            src[0, rows] = live * (-diff[0] - curve * t[1])
            src[1, rows] = live * (-diff[1] + curve * (t[5] - t[3]))
            src[2, rows] = live * (-diff[2] - 2.0 * curve * t[4])

    rims = (0, blocks - 1)
    middle = tuple(range(1, blocks - 1))

    def first(i, which, parts):
        def finish(c, rows, at, end):
            spad[c, i + 1, at : at + BLOCK] = end

        section(qpad, i, which, False, finish, parts)

    def force(i, which, parts):
        for j in parts:
            rows = slice(j * BLOCK, (j + 1) * BLOCK)
            at = top + j * BLOCK
            for c in which:
                if 1 <= c <= 3:
                    more = src[c - 1, rows]
                else:
                    more = mean[0, i, rows] * src[0, rows]
                    for k in range(1, 3):
                        more = more + mean[k, i, rows] * src[k, rows]
                old = spad[c, i + 1, at : at + BLOCK]
                spad[c, i + 1, at : at + BLOCK] = old + more

    def second(i, which, parts):
        def finish(c, rows, at, end):
            new[c, i, rows] = 0.5 * (qpad[c, i + 1, at : at + BLOCK] + end)

        section(spad, i, which, True, finish, parts)

    def at_edges(part, which, parts):
        def one(e, carry):
            part(e * (cells - 1), which, parts)
            return carry

        lax.fori_loop(0, 2, one, 0)

    def inside(part, parts, which=everything):
        def one(i, carry):
            part(i, which, parts)
            return carry

        lax.fori_loop(1, cells - 1, one, 0)

    step = reduce_y()
    for c in range(FIRST, comps):
        q_faces.append(q_face(c))
    span_wait(q_span)
    span_land(qpad, 0)
    load_visc.wait()
    early_face(0)
    early_face(1)
    early_send(0, (1, 0))
    early_send(1, (0,))
    inside(first, rims + middle)
    step = place(step)
    early_send(1, (1,))
    for c in range(2, comps - 1):
        early_face(c)
        early_send(c)
    for copy in q_faces[comps - 1]:
        copy.wait()
    at_edges(first, (comps - 1,), rims + middle)
    spread(*step)
    def force_halo(e, carry):
        for j in range(blocks):
            for c in range(1, comps - 1):
                at = top + j * BLOCK
                old = spad[c, e * (cells + 1), at : at + BLOCK]
                spad[c, e * (cells + 1), at : at + BLOCK] = old + src[c - 1, j * BLOCK : (j + 1) * BLOCK]
        return carry

    sources(rims)
    at_edges(force, moved + (comps - 1,), rims)
    inside(force, rims, moved + (comps - 1,))
    s_span = span_faces(spad, 1)
    sources(middle)
    at_edges(force, (comps - 1,), middle)
    last_faces = []
    for near in (right < left, right > left):
        w = jnp.where(near, 0, 1)
        last_faces.append(send(
            spad.at[comps - 1, jnp.where(near, cells, 1), inner],
            spad.at[comps - 1, jnp.where(near, 0, cells + 1), inner],
            hs_s.at[w, comps - 1], hs_r.at[w, comps - 1], (r, jnp.where(near, right, left), s),
        ))
    at_edges(force, moved, middle)
    inside(force, middle, moved + (comps - 1,))
    inside(second, middle)
    for m in range(6):
        for h in range(halves):
            rec_out[m, :, h * LANES : (h + 1) * LANES] = rec[m * halves + h]
    for copy in s_faces:
        copy.wait()
    lax.fori_loop(0, 2, force_halo, 0)
    at_edges(second, early, middle)
    span_wait(s_span)
    span_land(spad, 1)
    inside(second, rims)
    at_edges(second, early, rims)
    for copy, near in zip(last_faces, (right < left, right > left)):
        copy.wait()
        second(jnp.where(near, 0, cells - 1), (comps - 1,), rims + middle)


def store_kernel(a, b, a_out, b_out, sems):
    copies = [pltpu.make_async_copy(a, a_out, sems.at[0])]
    for c in range(b.shape[0]):
        copies.append(pltpu.make_async_copy(b.at[c], b_out.at[c], sems.at[1 + c]))
    for copy in copies:
        copy.start()
    for copy in copies:
        copy.wait()


def body(n_p, n_s, snapshots, snap_index, flow_state, eddy_viscosity, intersection, counts):
    start = flow_state[0]
    comps, cells, span, axial = start.shape
    halves = axial // LANES
    us = -(-6 * halves // n_p)
    units = us * n_p
    blocks = span // BLOCK
    tiles = span // ROWS_BF16
    n_x = 2 if n_p % 2 == 0 else 1
    n_y = n_p // n_x
    f32, i32 = jnp.float32, jnp.int32
    pad = (comps, cells + 2, span + 16, axial)
    vmem = pl.BlockSpec(memory_space=pltpu.VMEM)
    hbm = pl.BlockSpec(memory_space=pltpu.HBM)
    dma = pltpu.SemaphoreType.DMA
    operands = (snap_index, intersection[0], counts[0], snapshots[0], start, eddy_viscosity[0])
    operands = [pltpu.with_memory_space_constraint(a, pltpu.HBM) for a in operands]
    rec_shape = (6, span, axial)
    received, new = pl.pallas_call(
        functools.partial(couple_kernel, n_p, n_s, n_x, 1.0 / (SNAPS * cells * n_p)),
        out_shape=(pltpu.VMEM(rec_shape, f32), pltpu.VMEM(start.shape, f32)),
        in_specs=[hbm] * 6,
        out_specs=(vmem, vmem),
        scratch_shapes=[
            pltpu.SMEM(snap_index.shape, i32),
            pltpu.SMEM(intersection.shape[1:], i32),
            pltpu.SMEM(counts.shape[1:], i32),
            pltpu.VMEM((units, blocks, BLOCK, LANES), f32),
            pltpu.VMEM((n_y, us * n_x, blocks, BLOCK, LANES), f32),
            pltpu.VMEM((n_x, n_s, CAPACITY, us, BLOCK, LANES), f32),
            pltpu.VMEM((n_x, n_s, CAPACITY, us, BLOCK, LANES), f32),
            pltpu.VMEM((units, span, LANES), f32),
            pltpu.VMEM(pad, f32),
            pltpu.VMEM(pad, f32),
            pltpu.VMEM((2, comps - 1, span, axial), f32),
            pltpu.VMEM((3, cells, span, axial), f32),
            pltpu.VMEM((cells, span, axial), f32),
            pltpu.VMEM((span, axial), f32),
            pltpu.VMEM((3, span, axial), f32),
            pltpu.VMEM((2, 2, comps, cells, axial), f32),
            pltpu.VMEM((2, 2, comps, cells, axial), f32),
            dma((n_y, tiles)), dma((n_y, tiles)), dma((n_x, n_s)), dma((n_x, n_s)),
            dma((n_x, us)), dma((n_x, us)), dma((n_x, n_y, us)), dma((n_x, n_y, us)),
            dma((2, comps)), dma((2, comps)), dma((2, comps)), dma((2, comps)),
            dma((2, 2)), dma((2, 2)), dma((5,)), dma((tiles,)), pltpu.SemaphoreType.REGULAR,
        ]
        + [pltpu.VMEM((snapshots.shape[1], 3, cells, ROWS_BF16, axial), snapshots.dtype)] * tiles,
        compiler_params=pltpu.CompilerParams(
            collective_id=0, has_side_effects=True, vmem_limit_bytes=48 * 1024 * 1024
        ),
    )(*operands)
    results = [pltpu.with_memory_space_constraint(a, pltpu.VMEM) for a in (received, new)]
    received, new = pl.pallas_call(
        store_kernel,
        out_shape=(jax.ShapeDtypeStruct(rec_shape, f32), jax.ShapeDtypeStruct(start.shape, f32)),
        in_specs=[vmem, vmem],
        out_specs=(hbm, hbm),
        scratch_shapes=[dma((1 + comps,))],
    )(*results)
    return (received[None], new[None])


def solution(mesh):
    return jax.shard_map(
        functools.partial(body, mesh.shape["pitch"], mesh.shape["span"]),
        mesh=mesh,
        in_specs=(
            P("row", None, None, "pitch", "span", None),
            P(),
            P("row", None, "pitch", "span", None),
            P("row", "pitch", "span", None),
            P("row", None),
            P("row", None),
        ),
        out_specs=(P("row", None, "span", None), P("row", None, "pitch", "span", None)),
        check_vma=False,
    )
```

```python
import functools

import jax
import jax.numpy as jnp
from jax import lax
from jax.experimental import pallas as pl
from jax.experimental.pallas import tpu as pltpu
from jax.sharding import PartitionSpec as P

SNAPS = 16
BLOCK = 8
CAPACITY = 2
LANES = 128
FIRST = 5
ROWS_BF16 = 16
MESH = pl.DeviceIdType.MESH

stress_pairs = ((0, 0), (0, 1), (0, 2), (1, 1), (1, 2), (2, 2))
time_step = 0.1


def stress_tile(snaps, slots, mean, part, j):
    rows = slice(j * ROWS_BF16, (j + 1) * ROWS_BF16)
    cells = mean.shape[1]
    halves = mean.shape[3] // LANES
    for h in range(halves):
        cols = slice(h * LANES, (h + 1) * LANES)

        def one(i, acc):
            def load(t):
                return [snaps[slots[t], c, i, :, cols].astype(jnp.float32) for c in range(3)]

            base = load(0)
            sums, prods = None, None
            for t in range(1, SNAPS):
                now = load(t)
                d = [now[c] - base[c] for c in range(3)]
                pr = [d[p] * d[q] for p, q in stress_pairs]
                sums = d if sums is None else [a + b for a, b in zip(sums, d)]
                prods = pr if prods is None else [a + b for a, b in zip(prods, pr)]
            shift = [s * (1.0 / SNAPS) for s in sums]
            for c in range(3):
                mean[c, i, rows, cols] = base[c] + shift[c]
            return tuple(
                a + (pr - sums[p] * shift[q]) for a, pr, (p, q) in zip(acc, prods, stress_pairs)
            )

        zero = jnp.zeros((ROWS_BF16, LANES), jnp.float32)
        acc = lax.fori_loop(0, cells, one, (zero,) * 6)
        for m in range(6):
            for k in range(2):
                part[m * halves + h, 2 * j + k] = acc[m][k * BLOCK : (k + 1) * BLOCK]
    for u in range(6 * halves, part.shape[0]):
        for k in range(2):
            part[u, 2 * j + k] = jnp.zeros((BLOCK, LANES), jnp.float32)


def next_cell(x):
    lane = lax.broadcasted_iota(jnp.int32, x.shape, 1)
    return jnp.where(lane == x.shape[1] - 1, x, pltpu.roll(x, x.shape[1] - 1, 1))


def last_cell(x):
    lane = lax.broadcasted_iota(jnp.int32, x.shape, 1)
    return jnp.where(lane == 0, x, pltpu.roll(x, 1, 1))


def couple_kernel(
    n_p, n_s, n_x, scale,
    slots_hbm, links_hbm, counts_hbm, snaps_hbm, q_hbm, visc_hbm,
    rec_out, new,
    slot_list, links, counts,
    part, rsy, out_buf, a2a, rec, qpad, spad, face, mean, visc, dtm, src,
    zsend, zrecv,
    ry_s, ry_r, aa_s, aa_r, ax_s, ax_r, ay_s, ay_r, hq_s, hq_r, hs_s, hs_r, hz_s, hz_r,
    loc, snap_sem, later, *snaps,
):
    r, p, s = lax.axis_index("row"), lax.axis_index("pitch"), lax.axis_index("span")
    comps, cells, span, axial = q_hbm.shape
    n_y = n_p // n_x
    y, x = p // n_x, lax.rem(p, n_x)
    us = part.shape[0] // n_p
    ux = us * n_x
    blocks = span // BLOCK
    halves = axial // LANES
    tile = ROWS_BF16
    top = 8
    tiles = span // tile
    inner = pl.ds(top, span)

    snap_loads = [
        pltpu.make_async_copy(
            snaps_hbm.at[:, :, :, pl.ds(j * tile, tile)], snaps[j], snap_sem.at[j]
        )
        for j in range(tiles)
    ]
    snap_loads[0].start()
    barrier = pltpu.get_barrier_semaphore()

    def greet(*to):
        pl.semaphore_signal(barrier, inc=1, device_id=to, device_id_type=MESH)

    for d in range(1, n_p):
        greet(r, lax.rem(p + d, n_p), s)
    for d in range(n_y):
        greet(1 - r, lax.rem(y + d, n_y) * n_x + x, s)
    for d in range(1, n_s):
        @pl.when(s + d < n_s)
        def _():
            for e in range(n_x):
                greet(r, y * n_x + lax.rem(x + e, n_x), s + d)

    loads = []
    for k, (a, b) in enumerate(((slots_hbm, slot_list), (links_hbm, links), (counts_hbm, counts))):
        loads.append(pltpu.make_async_copy(a, b, loc.at[2 + k]))
    load_q = pltpu.make_async_copy(q_hbm, qpad.at[:, pl.ds(1, cells), inner], loc.at[0])
    load_visc = pltpu.make_async_copy(visc_hbm, visc, loc.at[1])
    for copy in loads:
        copy.start()
    for copy in snap_loads[1:]:
        copy.start()
    load_q.start()
    load_visc.start()

    pl.semaphore_wait(barrier, n_p - 1 + n_y + n_x * s)
    for d in range(1, n_s):
        @pl.when(s >= d)
        def _():
            for e in range(n_x):
                pl.semaphore_signal(
                    later, inc=1, device_id=(r, y * n_x + lax.rem(x + e, n_x), s - d),
                    device_id_type=MESH,
                )


    right, left = lax.rem(p + 1, n_p), lax.rem(p + n_p - 1, n_p)
    above, below = lax.rem(s + 1, n_s), lax.rem(s + n_s - 1, n_s)
    sides = ((cells - 1, 0, right), (0, cells + 1, left))

    def send(a, b, ss, rs, to):
        copy = pltpu.make_async_remote_copy(
            src_ref=a, dst_ref=b, send_sem=ss, recv_sem=rs, device_id=to, device_id_type=MESH
        )
        copy.start()
        return copy

    def q_face(c):
        return [
            send(q_hbm.at[c, mine], qpad.at[c, theirs, inner], hq_s.at[w, c], hq_r.at[w, c], (r, to, s))
            for w, (mine, theirs, to) in enumerate(sides)
        ]

    q_faces = [q_face(c) for c in range(FIRST)]

    span_sides = ((0, above, s < n_s - 1, s > 0), (1, below, s > 0, s < n_s - 1))
    for w, _, _, got in span_sides:
        @pl.when(jnp.logical_not(got))
        def _():
            for k in range(2):
                for c in range(comps):
                    zrecv[k, w, c] = jnp.zeros((cells, axial), jnp.float32)

    def span_faces(pad, k):
        def pack(i, carry):
            for c in range(comps):
                zsend[k, 0, c, pl.ds(i, 1)] = pad[c, i + 1, top + span - 1 : top + span]
                zsend[k, 1, c, pl.ds(i, 1)] = pad[c, i + 1, top : top + 1]
            return carry

        lax.fori_loop(0, cells, pack, 0)
        copies = []
        for w, to, sent, got in span_sides:
            copy = pltpu.make_async_remote_copy(
                src_ref=zsend.at[k, w], dst_ref=zrecv.at[k, w],
                send_sem=hz_s.at[k, w], recv_sem=hz_r.at[k, w],
                device_id=(r, p, to), device_id_type=MESH,
            )
            pl.when(sent)(copy.start)
            copies.append((copy, sent, got))
        return copies

    def span_wait(copies):
        for copy, sent, got in copies:
            pl.when(sent)(copy.wait_send)
            pl.when(got)(copy.wait_recv)

    def span_land(pad, k):
        def land(i, carry):
            for c in range(comps):
                pad[c, i + 1, top - 1 : top] = zrecv[k, 0, c, pl.ds(i, 1)]
                pad[c, i + 1, top + span : top + span + 1] = zrecv[k, 1, c, pl.ds(i, 1)]
            return carry

        lax.fori_loop(0, cells, land, 0)

    for copy in loads:
        copy.wait()

    slots = [slot_list[t] for t in range(SNAPS)]
    to_y = []
    for j in range(tiles):
        snap_loads[j].wait()
        stress_tile(snaps[j], slots, mean, part, j)
        pair = pl.ds(2 * j, 2)
        for d in range(n_y):
            to = lax.rem(y + d, n_y)
            to_y.append(send(
                part.at[pl.ds(to * ux, ux), pair], rsy.at[d, :, pair],
                ry_s.at[d, j], ry_r.at[d, j], (1 - r, to * n_x + x, s),
            ))

    for j in range(tiles):
        row = lax.broadcasted_iota(jnp.int32, (tile, axial), 0)
        first_count = counts[s * blocks + 2 * j]
        second_count = counts[s * blocks + 2 * j + 1]
        limit = jnp.where(row < BLOCK, first_count, second_count + BLOCK)
        dtm[j * tile : (j + 1) * tile] = jnp.where(row < limit, time_step, 0.0).astype(jnp.float32)
    load_q.wait()

    @pl.when(s < n_s - 1)
    def _():
        pl.semaphore_wait(later, n_x * (n_s - 1 - s))

    q_span = span_faces(qpad, 0)

    def section(pad, i, which, forced, finish, parts=tuple(range(blocks))):
        for j in parts:
            rows = slice(j * BLOCK, (j + 1) * BLOCK)
            nu = visc[i, rows]
            means = [mean[c, i, rows] for c in range(3 if forced and 4 in which else 1)]
            speed = 0.5 + means[0]
            live = dtm[rows]
            ahead = live * (nu - 0.5 * next_cell(speed))
            behind = live * (nu + 0.5 * last_cell(speed))
            nu = live * nu
            at = top + j * BLOCK
            ends = []
            for c in which:
                x = pad[c, i + 1, at : at + BLOCK]
                around = (
                    pad[c, i, at : at + BLOCK] + pad[c, i + 2, at : at + BLOCK]
                    + pad[c, i + 1, at - 1 : at + BLOCK - 1]
                    + pad[c, i + 1, at + 1 : at + BLOCK + 1]
                )
                step = (
                    ahead * next_cell(x) + behind * last_cell(x) + nu * (around - 6.0 * x)
                )
                if forced and 1 <= c <= 3:
                    step = step + src[c - 1, rows]
                if forced and c == 4:
                    step = step + (
                        means[0] * src[0, rows] + means[1] * src[1, rows] + means[2] * src[2, rows]
                    )
                ends.append(x + step)
            for c, end in zip(which, ends):
                finish(c, rows, at, end)

    everything = tuple(range(comps))
    early = tuple(range(comps - 1))
    moved = early[1:]
    s_faces = []

    def early_face(c):
        for copy in q_faces[c]:
            copy.wait()

        def one(e, carry):
            i = e * (cells - 1)

            def finish(c, rows, at, end):
                face[e, c, rows] = end
                spad[c, i + 1, at : at + BLOCK] = end

            section(qpad, i, (c,), False, finish)
            return carry

        lax.fori_loop(0, 2, one, 0)

    def early_send(c, chosen=(0, 1)):
        for w in chosen:
            mine, theirs, to = sides[w]
            s_faces.append(send(
                face.at[1 - w, c], spad.at[c, theirs, inner],
                hs_s.at[w, c], hs_r.at[w, c], (r, to, s),
            ))

    def reduce_y():
        for copy in to_y:
            copy.wait()
        exchange = []
        for d in range(n_s):
            to = lax.rem(s + d, n_s)
            count = jnp.int32(0)
            picks = [jnp.int32(0)] * CAPACITY
            for k in range(blocks):
                block = links[to * blocks + k]
                here = block // blocks == s
                inside = block % blocks
                for c in range(CAPACITY):
                    picks[c] = jnp.where(here & (count == c), inside, picks[c])
                count = count + here.astype(jnp.int32)
            for e in range(n_x):
                to_x = lax.rem(x + e, n_x)
                local = d == 0 and e == 0
                for c in range(CAPACITY):
                    for u in range(us):
                        total = rsy[0, to_x * us + u, picks[c]]
                        for f in range(1, n_y):
                            total = total + rsy[f, to_x * us + u, picks[c]]
                        if local:
                            a2a[0, 0, c, u] = total * scale
                        else:
                            out_buf[e, d, c, u] = total * scale
                if not local:
                    exchange.append(send(
                        out_buf.at[e, d], a2a.at[e, d], aa_s.at[e, d], aa_r.at[e, d],
                        (r, y * n_x + to_x, to),
                    ))
        return exchange

    def place(exchange):
        sources = [links[s * blocks + k] // blocks for k in range(blocks)]
        for copy in exchange:
            copy.wait()
        for k in range(blocks):
            slot = jnp.int32(0)
            for e in range(k):
                slot = slot + (sources[e] == sources[k]).astype(jnp.int32)
            slot = jnp.minimum(slot, CAPACITY - 1)
            away = lax.rem(s - sources[k] + n_s, n_s)
            for u in range(us):
                total = a2a[0, away, slot, u]
                for e in range(1, n_x):
                    total = total + a2a[e, away, slot, u]
                rec[p * us + u, k * BLOCK : (k + 1) * BLOCK] = total
        over_x, over_y = [], []
        for u in range(us):
            mine = pl.ds(p * us + u, 1)
            for d in range(1, n_x):
                to = y * n_x + lax.rem(x + d, n_x)
                over_x.append(send(
                    rec.at[mine], rec.at[mine], ax_s.at[d, u], ax_r.at[d, u], (r, to, s)
                ))
        mine = pl.ds(p * us, us)
        for d in range(1, n_y):
            to = lax.rem(y + d, n_y) * n_x + x
            over_y.append(send(
                rec.at[mine], rec.at[mine], ay_s.at[0, d, 0], ay_r.at[0, d, 0], (r, to, s)
            ))
        return over_x, over_y

    def spread(over_x, over_y):
        for u in range(us):
            for d in range(1, n_x):
                over_x[u * (n_x - 1) + d - 1].wait()
                got = pl.ds((y * n_x + lax.rem(x + n_x - d, n_x)) * us + u, 1)
                for e in range(1, n_y):
                    to = lax.rem(y + e, n_y) * n_x + x
                    over_y.append(send(
                        rec.at[got], rec.at[got], ay_s.at[d, e, u], ay_r.at[d, e, u], (r, to, s)
                    ))
        for copy in over_y:
            copy.wait()

    def sources(parts):
        for j in parts:
            rows = slice(j * BLOCK, (j + 1) * BLOCK)
            t = [
                jnp.concatenate([rec[m * halves + h, rows] for h in range(halves)], axis=1)
                for m in range(6)
            ]
            row = lax.broadcasted_iota(jnp.int32, (BLOCK, axial), 0) + (s * span + j * BLOCK)
            curve = 1.0 / (1.0 + (row.astype(jnp.float32) + 0.5) / (span * n_s))
            diff = [(next_cell(t[m]) - last_cell(t[m])) * 0.5 for m in range(3)]
            live = dtm[rows]
            src[0, rows] = live * (-diff[0] - curve * t[1])
            src[1, rows] = live * (-diff[1] + curve * (t[5] - t[3]))
            src[2, rows] = live * (-diff[2] - 2.0 * curve * t[4])

    rims = (0, blocks - 1)
    middle = tuple(range(1, blocks - 1))

    def first(i, which, parts):
        def finish(c, rows, at, end):
            spad[c, i + 1, at : at + BLOCK] = end

        section(qpad, i, which, False, finish, parts)

    def force(i, which, parts):
        for j in parts:
            rows = slice(j * BLOCK, (j + 1) * BLOCK)
            at = top + j * BLOCK
            for c in which:
                if 1 <= c <= 3:
                    more = src[c - 1, rows]
                else:
                    more = mean[0, i, rows] * src[0, rows]
                    for k in range(1, 3):
                        more = more + mean[k, i, rows] * src[k, rows]
                old = spad[c, i + 1, at : at + BLOCK]
                spad[c, i + 1, at : at + BLOCK] = old + more

    def second(i, which, parts):
        def finish(c, rows, at, end):
            new[c, i, rows] = 0.5 * (qpad[c, i + 1, at : at + BLOCK] + end)

        section(spad, i, which, True, finish, parts)

    def at_edges(part, which, parts):
        def one(e, carry):
            part(e * (cells - 1), which, parts)
            return carry

        lax.fori_loop(0, 2, one, 0)

    def inside(part, parts, which=everything):
        def one(i, carry):
            part(i, which, parts)
            return carry

        lax.fori_loop(1, cells - 1, one, 0)

    step = reduce_y()
    for c in range(FIRST, comps):
        q_faces.append(q_face(c))
    span_wait(q_span)
    span_land(qpad, 0)
    load_visc.wait()
    early_face(0)
    early_face(1)
    early_send(0, (1, 0))
    early_send(1, (0,))
    inside(first, rims + middle)
    step = place(step)
    early_send(1, (1,))
    for c in range(2, comps - 1):
        early_face(c)
        early_send(c)
    for copy in q_faces[comps - 1]:
        copy.wait()
    at_edges(first, (comps - 1,), rims + middle)
    spread(*step)
    def force_halo(e, carry):
        for j in range(blocks):
            for c in range(1, comps - 1):
                at = top + j * BLOCK
                old = spad[c, e * (cells + 1), at : at + BLOCK]
                spad[c, e * (cells + 1), at : at + BLOCK] = old + src[c - 1, j * BLOCK : (j + 1) * BLOCK]
        return carry

    sources(rims)
    at_edges(force, moved + (comps - 1,), rims)
    inside(force, rims, moved + (comps - 1,))
    s_span = span_faces(spad, 1)
    sources(middle)
    at_edges(force, (comps - 1,), middle)
    last_faces = []
    for near in (right < left, right > left):
        w = jnp.where(near, 0, 1)
        last_faces.append(send(
            spad.at[comps - 1, jnp.where(near, cells, 1), inner],
            spad.at[comps - 1, jnp.where(near, 0, cells + 1), inner],
            hs_s.at[w, comps - 1], hs_r.at[w, comps - 1], (r, jnp.where(near, right, left), s),
        ))
    at_edges(force, moved, middle)
    inside(force, middle, moved + (comps - 1,))
    inside(second, middle)
    for m in range(6):
        for h in range(halves):
            rec_out[m, :, h * LANES : (h + 1) * LANES] = rec[m * halves + h]
    for copy in s_faces:
        copy.wait()
    lax.fori_loop(0, 2, force_halo, 0)
    at_edges(second, early, middle)
    span_wait(s_span)
    span_land(spad, 1)
    inside(second, rims)
    at_edges(second, early, rims)
    for copy, near in zip(last_faces, (right < left, right > left)):
        copy.wait()
        second(jnp.where(near, 0, cells - 1), (comps - 1,), rims + middle)


def store_kernel(a, b, a_out, b_out, sems):
    copies = [pltpu.make_async_copy(a, a_out, sems.at[0])]
    for c in range(b.shape[0]):
        copies.append(pltpu.make_async_copy(b.at[c], b_out.at[c], sems.at[1 + c]))
    for copy in copies:
        copy.start()
    for copy in copies:
        copy.wait()


def body(n_p, n_s, snapshots, snap_index, flow_state, eddy_viscosity, intersection, counts):
    start = flow_state[0]
    comps, cells, span, axial = start.shape
    halves = axial // LANES
    us = -(-6 * halves // n_p)
    units = us * n_p
    blocks = span // BLOCK
    tiles = span // ROWS_BF16
    n_x = 2 if n_p % 2 == 0 else 1
    n_y = n_p // n_x
    f32, i32 = jnp.float32, jnp.int32
    pad = (comps, cells + 2, span + 16, axial)
    vmem = pl.BlockSpec(memory_space=pltpu.VMEM)
    hbm = pl.BlockSpec(memory_space=pltpu.HBM)
    dma = pltpu.SemaphoreType.DMA
    operands = (snap_index, intersection[0], counts[0], snapshots[0], start, eddy_viscosity[0])
    operands = [pltpu.with_memory_space_constraint(a, pltpu.HBM) for a in operands]
    rec_shape = (6, span, axial)
    received, new = pl.pallas_call(
        functools.partial(couple_kernel, n_p, n_s, n_x, 1.0 / (SNAPS * cells * n_p)),
        out_shape=(pltpu.VMEM(rec_shape, f32), pltpu.VMEM(start.shape, f32)),
        in_specs=[hbm] * 6,
        out_specs=(vmem, vmem),
        scratch_shapes=[
            pltpu.SMEM(snap_index.shape, i32),
            pltpu.SMEM(intersection.shape[1:], i32),
            pltpu.SMEM(counts.shape[1:], i32),
            pltpu.VMEM((units, blocks, BLOCK, LANES), f32),
            pltpu.VMEM((n_y, us * n_x, blocks, BLOCK, LANES), f32),
            pltpu.VMEM((n_x, n_s, CAPACITY, us, BLOCK, LANES), f32),
            pltpu.VMEM((n_x, n_s, CAPACITY, us, BLOCK, LANES), f32),
            pltpu.VMEM((units, span, LANES), f32),
            pltpu.VMEM(pad, f32),
            pltpu.VMEM(pad, f32),
            pltpu.VMEM((2, comps - 1, span, axial), f32),
            pltpu.VMEM((3, cells, span, axial), f32),
            pltpu.VMEM((cells, span, axial), f32),
            pltpu.VMEM((span, axial), f32),
            pltpu.VMEM((3, span, axial), f32),
            pltpu.VMEM((2, 2, comps, cells, axial), f32),
            pltpu.VMEM((2, 2, comps, cells, axial), f32),
            dma((n_y, tiles)), dma((n_y, tiles)), dma((n_x, n_s)), dma((n_x, n_s)),
            dma((n_x, us)), dma((n_x, us)), dma((n_x, n_y, us)), dma((n_x, n_y, us)),
            dma((2, comps)), dma((2, comps)), dma((2, comps)), dma((2, comps)),
            dma((2, 2)), dma((2, 2)), dma((5,)), dma((tiles,)), pltpu.SemaphoreType.REGULAR,
        ]
        + [pltpu.VMEM((snapshots.shape[1], 3, cells, ROWS_BF16, axial), snapshots.dtype)] * tiles,
        compiler_params=pltpu.CompilerParams(
            collective_id=0, has_side_effects=True, vmem_limit_bytes=48 * 1024 * 1024
        ),
    )(*operands)
    results = [pltpu.with_memory_space_constraint(a, pltpu.VMEM) for a in (received, new)]
    received, new = pl.pallas_call(
        store_kernel,
        out_shape=(jax.ShapeDtypeStruct(rec_shape, f32), jax.ShapeDtypeStruct(start.shape, f32)),
        in_specs=[vmem, vmem],
        out_specs=(hbm, hbm),
        scratch_shapes=[dma((1 + comps,))],
    )(*results)
    return (received[None], new[None])


def solution(mesh):
    return jax.shard_map(
        functools.partial(body, mesh.shape["pitch"], mesh.shape["span"]),
        mesh=mesh,
        in_specs=(
            P("row", None, None, "pitch", "span", None),
            P(),
            P("row", None, "pitch", "span", None),
            P("row", "pitch", "span", None),
            P("row", None),
            P("row", None),
        ),
        out_specs=(P("row", None, "span", None), P("row", None, "pitch", "span", None)),
        check_vma=False,
    )
```
